32 devices in a mesh: shard: 2 (over core), ctx: 4 (over y, x), tp: 4 (over z).
Axes of the slice: x: 2, y: 2, z: 4, core: 2. Of those that a mesh axis runs over, the one named last changes fastest.
Arguments:
- inputs: bfloat16 [4, 2048, 1536], P('shard', 'ctx'), may hold values from -6 to 6
- starts: int32 [4, 2], P('shard'), may hold values from 0 to 1792, as said below
- first_gain: bfloat16 [1536], P(('shard', 'ctx')), may hold values from 0.099609375 to 1.8984375
- query_weight: bfloat16 [1536, 1536], P(('shard', 'ctx'), 'tp'), may hold values from -0.15625 to 0.15625
- key_matrix: bfloat16 [1536, 768], P(('shard', 'ctx'), 'tp'), may hold values from -0.15625 to 0.15625
- value_matrix: bfloat16 [1536, 768], P(('shard', 'ctx'), 'tp'), may hold values from -0.15625 to 0.15625
- out_weight: bfloat16 [1536, 1536], P('tp', ('shard', 'ctx')), may hold values from -2.5 to 2.5
- second_gain: bfloat16 [1536], P(('shard', 'ctx')), may hold values from 0.099609375 to 1.8984375
- gate_weight: bfloat16 [1536, 4096], P(('shard', 'ctx'), 'tp'), may hold values from -0.15625 to 0.15625
- up_weight: bfloat16 [1536, 4096], P(('shard', 'ctx'), 'tp'), may hold values from -0.15625 to 0.15625
- down_weight: bfloat16 [4096, 1536], P('tp', ('shard', 'ctx')), may hold values from -0.375 to 0.375
- grad_out: bfloat16 [4, 2048, 1536], P('shard', 'ctx'), may hold values from -6 to 6
Outputs:
- outputs: bfloat16 [4, 2048, 1536], P('shard', 'ctx')
- grad_inputs: bfloat16 [4, 2048, 1536], P('shard', 'ctx')
- grad_first_gain: float32 [1536], P(('shard', 'ctx'))
- grad_query_weight: float32 [1536, 1536], P(('shard', 'ctx'), 'tp')
- grad_key_weight: float32 [1536, 768], P(('shard', 'ctx'), 'tp')
- grad_value_weight: float32 [1536, 768], P(('shard', 'ctx'), 'tp')
- grad_out_weight: float32 [1536, 1536], P('tp', ('shard', 'ctx'))
- grad_second_gain: float32 [1536], P(('shard', 'ctx'))
- grad_gate_weight: float32 [1536, 4096], P(('shard', 'ctx'), 'tp')
- grad_up_weight: float32 [1536, 4096], P(('shard', 'ctx'), 'tp')
- grad_down_weight: float32 [4096, 1536], P('tp', ('shard', 'ctx'))
The draws below stay inside these ranges and needn't reach their ends.
Inputs may be any that keep to these rules, and one draw needn't show every extreme that they name: `starts`: each sequence's 2 image pieces of 256 tokens start in increasing order, do not intersect and lie inside the sequence.
All inputs are finite; a program needn't handle non-finite values.
Results may differ from the reference program's by a relative error of at most 0.025.
Values may be sent and summed in bfloat16 or wider, within the bound.
No kernel may reach another device: no remote copies, remote signals or barrier semaphores. Data moves between devices by JAX's collectives and lax.ppermute only.
A program may use at most 192 MiB of HBM per device.

```python
import math
import jax
import jax.numpy as jnp
from jax import lax

MODEL_DIMENSION = 1536
QUERY_HEADS = 16
KEY_VALUE_HEADS = 8
HEAD_SIZE = 96
FF = 4096
PIECE = 256
LEN = 2048
SEQS = 4
N_TP = 4


def draw_starts(key, part):
    first_key = jax.random.fold_in(key, 11)
    second_key = jax.random.fold_in(key, 12)
    first_start = jax.random.randint(first_key, (SEQS,), 0, LEN - 2 * PIECE + 1)
    second_start = jax.random.randint(second_key, (SEQS,), first_start + PIECE, LEN - PIECE + 1)
    return jnp.stack([first_start, second_start], axis=1).astype(jnp.int32)


def level_of(rng, shape, shards, low, high):
    factor_of, own = 1.0, jax.random.fold_in(rng, 6)
    for dim, parts in shards:
        steps = jnp.exp(jax.random.uniform(jax.random.fold_in(own, dim), (parts,), jnp.float32, low / len(shards), high / len(shards)))
        factor_of = factor_of * jnp.repeat(steps, shape[dim] // parts).reshape([-1 if axis == dim else 1 for axis in range(len(shape))])
    return factor_of


def scatter_about(key, dims, scale, reach, cuts=(), held_as=jnp.bfloat16):
    array = jax.random.normal(key, dims, jnp.float32) * scale
    if len(cuts) > 0:
        array = level_of(key, dims, cuts, -0.22, 0.18) * array
    return jnp.clip(array, min=-reach, max=reach).astype(held_as)


def setup_inputs(seed: int = 0) -> dict:
    keys = jax.random.split(jax.random.key(seed), 13)
    return {
        "inputs": scatter_about(keys[0], (SEQS, LEN, MODEL_DIMENSION), 1.0, 6.0, ((0, 2), (1, 4))),
        "starts": draw_starts(jax.random.fold_in(keys[12], 71), 0),
        "first_gain": jnp.clip(1.0 + 0.18 * jax.random.normal(keys[2], (MODEL_DIMENSION,), jnp.float32), 0.099609375, 1.8984375).astype(jnp.bfloat16),
        "query_weight": scatter_about(keys[3], (MODEL_DIMENSION, QUERY_HEADS * HEAD_SIZE), MODEL_DIMENSION ** -0.5, 0.15625, ((0, 8), (1, 4))),
        "key_matrix": scatter_about(keys[4], (MODEL_DIMENSION, KEY_VALUE_HEADS * HEAD_SIZE), MODEL_DIMENSION ** -0.5, 0.15625, ((0, 8), (1, 4))),
        "value_matrix": scatter_about(keys[5], (MODEL_DIMENSION, KEY_VALUE_HEADS * HEAD_SIZE), MODEL_DIMENSION ** -0.5, 0.15625, ((0, 8), (1, 4))),
        "out_weight": scatter_about(keys[6], (QUERY_HEADS * HEAD_SIZE, MODEL_DIMENSION), (max(QUERY_HEADS * HEAD_SIZE // 256, 1)) ** -0.5, 2.5, ((0, 4), (1, 8))),
        "second_gain": jnp.clip(1.0 + 0.18 * jax.random.normal(keys[7], (MODEL_DIMENSION,), jnp.float32), 0.099609375, 1.8984375).astype(jnp.bfloat16),
        "gate_weight": scatter_about(keys[8], (MODEL_DIMENSION, FF), MODEL_DIMENSION ** -0.5, 0.15625, ((0, 8), (1, 4))),
        "up_weight": scatter_about(keys[9], (MODEL_DIMENSION, FF), MODEL_DIMENSION ** -0.5, 0.15625, ((0, 8), (1, 4))),
        "down_weight": scatter_about(keys[10], (FF, MODEL_DIMENSION), (max(FF // 16, 1)) ** -0.5, 0.375, ((0, 4), (1, 8))),
        "grad_out": scatter_about(keys[11], (SEQS, LEN, MODEL_DIMENSION), 1.0, 6.0, ((0, 2), (1, 4))),
    }


@jax.custom_vjp
def reduced_precision(v):
    return lax.optimization_barrier(v.astype(jnp.bfloat16)).astype(jnp.float32)

@jax.custom_vjp
def low_back(v):
    return v

def low_keep(v):
    return (reduced_precision(v), None)

def low_pass(kept, grad):
    return (grad,)

def back_keep(v):
    return (v, None)

def back_low(kept, grad):
    return (reduced_precision(grad),)
reduced_precision.defvjp(low_keep, low_pass)
low_back.defvjp(back_keep, back_low)
EPSILON = 1e-05
ROPE_BASE = 100000.0
NEGATIVE = -1e+30

def rotation_tables(positions, head_dim):
    half_width = head_dim // 2
    inverse = jnp.exp(jnp.arange(half_width, dtype=jnp.float32) * (-2.0 * math.log(ROPE_BASE) / head_dim))
    angles = positions.astype(jnp.float32)[:, None] * inverse[None, :]
    return (jnp.cos(angles)[:, None, :], jnp.sin(angles)[:, None, :])

def apply_rotary_heads(tensor, cosine_lookup, sine_lookup):
    half_width = tensor.shape[-1] // 2
    front_half = tensor[..., :half_width]
    back_half = tensor[..., half_width:]
    return jnp.concatenate([front_half * cosine_lookup - back_half * sine_lookup, back_half * cosine_lookup + front_half * sine_lookup], axis=-1)

def piece_number(positions, start_row):
    inside = (positions[:, None] >= start_row[None, :]) & (positions[:, None] < start_row[None, :] + PIECE)
    labels = jnp.arange(1, start_row.shape[0] + 1, dtype=jnp.int32)
    return lax.optimization_barrier(jnp.sum(jnp.where(inside, labels[None, :], 0), axis=1))

def allowed_mask(query_pos, key_pos, start_row):
    query_piece = piece_number(query_pos, start_row)
    key_piece = piece_number(key_pos, start_row)
    causal = key_pos[None, :] <= query_pos[:, None]
    same_piece = (query_piece[:, None] == key_piece[None, :]) & (query_piece[:, None] > 0)
    return causal | same_piece

def layer_forward(stream, first_gain, query_weight, key_matrix, value_matrix, out_weight, second_gain, gate_weight, up_weight, down_weight, allowed, cosine_lookup, sine_lookup):
    highest = lax.Precision.HIGHEST
    count_of_rows = stream.shape[0]
    inverse_one = lax.rsqrt(lax.optimization_barrier(jnp.mean(stream * stream, axis=-1, keepdims=True)) + EPSILON)
    normed_one = reduced_precision(stream * inverse_one * first_gain)
    query_pre = low_back(jnp.dot(normed_one, query_weight, precision=highest))
    key_unrotated = low_back(jnp.dot(normed_one, key_matrix, precision=highest))
    value_row_matrix = reduced_precision(low_back(jnp.dot(normed_one, value_matrix, precision=highest)))
    query_rotated = reduced_precision(apply_rotary_heads(query_pre.reshape(count_of_rows, QUERY_HEADS, HEAD_SIZE), cosine_lookup, sine_lookup))
    key_rotated = reduced_precision(apply_rotary_heads(key_unrotated.reshape(count_of_rows, KEY_VALUE_HEADS, HEAD_SIZE), cosine_lookup, sine_lookup))
    value_per_head = value_row_matrix.reshape(count_of_rows, KEY_VALUE_HEADS, HEAD_SIZE)
    query_grouped = query_rotated.reshape(count_of_rows, KEY_VALUE_HEADS, QUERY_HEADS // KEY_VALUE_HEADS, HEAD_SIZE)
    scores = low_back(jnp.einsum('qgrd,kgd->grqk', query_grouped, key_rotated, precision=highest) * HEAD_SIZE ** (-0.5))
    masked = jnp.where(allowed, scores, NEGATIVE)
    top_score = lax.optimization_barrier(jnp.max(masked, axis=-1, keepdims=True))
    exp_scores = jnp.exp(masked - top_score)
    softmax_out = exp_scores / lax.optimization_barrier(jnp.sum(exp_scores, axis=-1, keepdims=True))
    mixed_heads = jnp.einsum('grqk,kgd->qgrd', reduced_precision(softmax_out), value_per_head, precision=highest)
    mixed_low = reduced_precision(low_back(mixed_heads.reshape(count_of_rows, QUERY_HEADS * HEAD_SIZE)))
    attn_terms = jnp.einsum('tjc,jcd->jtd', mixed_low.reshape(count_of_rows, N_TP, QUERY_HEADS * HEAD_SIZE // N_TP), out_weight.reshape(N_TP, QUERY_HEADS * HEAD_SIZE // N_TP, MODEL_DIMENSION), precision=highest)
    attn_sum = low_back(lax.optimization_barrier(jnp.sum(reduced_precision(attn_terms), axis=0)))
    middle = stream + attn_sum
    inverse_two = lax.rsqrt(lax.optimization_barrier(jnp.mean(middle * middle, axis=-1, keepdims=True)) + EPSILON)
    normed_two = reduced_precision(middle * inverse_two * second_gain)
    gate_pre = low_back(jnp.dot(normed_two, gate_weight, precision=highest))
    up_pre = low_back(jnp.dot(normed_two, up_weight, precision=highest))
    hidden_low = reduced_precision(jax.nn.silu(gate_pre) * up_pre)
    ffn_terms = jnp.einsum('tjc,jcd->jtd', hidden_low.reshape(count_of_rows, N_TP, FF // N_TP), down_weight.reshape(N_TP, FF // N_TP, MODEL_DIMENSION), precision=highest)
    return middle + lax.optimization_barrier(jnp.sum(reduced_precision(ffn_terms), axis=0))

def reference(inputs, starts, first_gain, query_weight, key_matrix, value_matrix, out_weight, second_gain, gate_weight, up_weight, down_weight, grad_out):
    weights = tuple((w_item.astype(jnp.float32) for w_item in (first_gain, query_weight, key_matrix, value_matrix, out_weight, second_gain, gate_weight, up_weight, down_weight)))
    positions = jnp.arange(LEN, dtype=jnp.int32)
    cosine_lookup, sine_lookup = rotation_tables(positions, HEAD_SIZE)

    def one_sequence(running, operands):
        seq_inputs, seq_grads, start_row = operands
        allowed = allowed_mask(positions, positions, start_row)

        def forward_fn(stream, *weight_items):
            return layer_forward(stream, *weight_items, allowed, cosine_lookup, sine_lookup)
        result, pullback = jax.vjp(forward_fn, seq_inputs.astype(jnp.float32), *weights)
        gradients = pullback(seq_grads.astype(jnp.float32))
        updated = tuple((total + piece for total, piece in zip(running, gradients[1:])))
        return (updated, (result.astype(jnp.bfloat16), gradients[0].astype(jnp.bfloat16)))
    initial = tuple((jnp.zeros(w_item.shape, jnp.float32) for w_item in weights))
    totals, (outputs, grad_inputs) = lax.scan(one_sequence, initial, (inputs, grad_out, starts))
    return (outputs, grad_inputs, totals[0], totals[1], totals[2], totals[3], totals[4], totals[5], totals[6], totals[7], totals[8])
```

```python
import functools
import math

import jax
import jax.numpy as jnp
from jax import lax
from jax.experimental import pallas as pl
from jax.experimental.pallas import tpu as pltpu
from jax.sharding import PartitionSpec as P

HEAD_SIZE = 96
PIECE = 256

EPSILON = 1e-05
ROPE_BASE = 100000.0
NEGATIVE = -1e30
F32 = jnp.float32
BF16 = jnp.bfloat16
LANES = 128
VMEM_LIMIT=56<<20

def nt(left, right):
    return lax.dot_general(left, right, (((1,), (1,)), ((), ())), preferred_element_type=F32)
def nn(left, right):
    return jnp.dot(left, right, preferred_element_type=F32)

def head_pair(block, group, repeat):
    first = group * repeat
    return jnp.concatenate(
        [block[:, (first + r) * HEAD_SIZE : (first + r + 1) * HEAD_SIZE] for r in range(repeat)], axis=0)

def side_by_side(groups, repeat, tile):
    return jnp.concatenate([g[r * tile : (r + 1) * tile] for g in groups for r in range(repeat)], axis=1)

def attend_kernel(n_groups, repeat, n_blocks, block, bases_ref, q_ref, kv_ref, limit_ref, mixed_ref, lse_ref, k_s, vt_s):
    tile = q_ref.shape[1]
    cols = repeat * tile
    kv_width = n_groups * HEAD_SIZE
    factor = HEAD_SIZE ** (-0.5) * math.log2(math.e)

    @pl.when(pl.program_id(1) == 0)
    def _():
        for g in range(n_groups):
            k_s[g] = kv_ref[0, :, g * HEAD_SIZE : (g + 1) * HEAD_SIZE]
            vt_s[g] = kv_ref[0, :, kv_width + g * HEAD_SIZE : kv_width + (g + 1) * HEAD_SIZE].T

    limit = jnp.concatenate([limit_ref[0, 0]] * repeat, axis=1)
    offset = lax.broadcasted_iota(jnp.int32, (block, cols), 0)
    results = []
    for g in range(n_groups):
        q = head_pair(q_ref[0], g, repeat)
        blocks = []
        for j in range(n_blocks):
            scores = nt(k_s[g, j * block : (j + 1) * block, :], q) * factor
            blocks.append(jnp.where(offset <= limit - bases_ref[j], scores, NEGATIVE))
        top = functools.reduce(jnp.maximum, [jnp.max(x, axis=0, keepdims=True) for x in blocks])
        total = jnp.zeros((1, cols), F32)
        acc = jnp.zeros((HEAD_SIZE, cols), F32)
        for j in range(n_blocks):
            probs = jnp.exp2(blocks[j] - top)
            total = total + jnp.sum(probs, axis=0, keepdims=True)
            acc = acc + nn(vt_s[g, :, j * block : (j + 1) * block], probs.astype(BF16))
        lse_ref[0, 0, g : g + 1, :] = top + jnp.log2(total)
        results.append((acc / total).T)
    mixed_ref[0] = side_by_side(results, repeat, tile).astype(BF16)

def attend(query, kv_all, limits, bases, tile=128):
    seqs, toks, q_width = query.shape
    length = kv_all.shape[1]
    n_groups = kv_all.shape[2] // (2 * HEAD_SIZE)
    repeat = q_width // HEAD_SIZE // n_groups
    n_blocks = bases.shape[0]
    block = length // n_blocks
    n_tiles = toks // tile
    return pl.pallas_call(
        functools.partial(attend_kernel, n_groups, repeat, n_blocks, block),
        grid_spec=pltpu.PrefetchScalarGridSpec(
            num_scalar_prefetch=1,
            grid=(seqs, n_tiles),
            in_specs=[
                pl.BlockSpec((1, tile, q_width), lambda b, t, _: (b, t, 0)),
                pl.BlockSpec((1, length, kv_all.shape[2]), lambda b, t, _: (b, 0, 0)),
                pl.BlockSpec((1, 1, 1, tile), lambda b, t, _: (b, t, 0, 0)),
            ],
            out_specs=[
                pl.BlockSpec((1, tile, q_width), lambda b, t, _: (b, t, 0)),
                pl.BlockSpec((1, 1, n_groups, repeat * tile), lambda b, t, _: (b, t, 0, 0)),
            ],
            scratch_shapes=[
                pltpu.VMEM((n_groups, length, HEAD_SIZE), BF16),
                pltpu.VMEM((n_groups, HEAD_SIZE, length), BF16),
            ],
        ),
        out_shape=[
            jax.ShapeDtypeStruct((seqs, toks, q_width), BF16),
            jax.ShapeDtypeStruct((seqs, n_tiles, n_groups, repeat * tile), F32),
        ],
        compiler_params=pltpu.CompilerParams(vmem_limit_bytes=VMEM_LIMIT),
        cost_estimate=pl.CostEstimate(
            flops=4 * seqs * toks * length * 256 * n_groups * repeat,
            bytes_accessed=4 * seqs * toks * q_width + 4 * seqs * length * q_width,
            transcendentals=seqs * toks * length * n_groups * repeat),
        name="attend",
    )(bases, query, kv_all, limits)

def turn(value, cosine, sine):
    half = HEAD_SIZE // 2
    width = value.shape[-1]
    lane = lax.broadcasted_iota(jnp.int32, value.shape, 1) % HEAD_SIZE
    other = jnp.where(lane < half, pltpu.roll(value, width - half, 1), pltpu.roll(value, half, 1))
    return value * cosine + other * sine

def attend_back_kernel(n_groups, repeat, n_blocks, block, bases_ref, q_ref, kv_ref, limit_ref, lse_ref, mixed_ref,
                       grad_ref, cos_ref, sin_ref, dq_ref, dkv_ref, k_s, v_s, kt_s, dk_s, dv_s):
    tile = q_ref.shape[1]
    cols = repeat * tile
    kv_width = n_groups * HEAD_SIZE
    scale = HEAD_SIZE ** (-0.5)
    factor = scale * math.log2(math.e)

    @pl.when(pl.program_id(1) == 0)
    def _():
        for g in range(n_groups):
            k = kv_ref[0, :, g * HEAD_SIZE : (g + 1) * HEAD_SIZE]
            k_s[g] = k
            kt_s[g] = k.T
            v_s[g] = kv_ref[0, :, kv_width + g * HEAD_SIZE : kv_width + (g + 1) * HEAD_SIZE]
        dk_s[...] = jnp.zeros_like(dk_s)
        dv_s[...] = jnp.zeros_like(dv_s)

    limit = jnp.concatenate([limit_ref[0, 0]] * repeat, axis=1)
    offset = lax.broadcasted_iota(jnp.int32, (block, cols), 0)
    ones = jnp.ones((8, HEAD_SIZE), BF16)
    results = []
    for g in range(n_groups):
        q = head_pair(q_ref[0], g, repeat)
        grad = head_pair(grad_ref[0], g, repeat)
        mixed = head_pair(mixed_ref[0], g, repeat)
        product = grad.astype(F32) * mixed.astype(F32)
        high = product.astype(BF16)
        low = (product - high.astype(F32)).astype(BF16)
        delta = (nt(ones, high) + nt(ones, low))[0:1]
        lse = lse_ref[0, 0, g : g + 1, :]
        dqt = jnp.zeros((HEAD_SIZE, cols), F32)
        for j in range(n_blocks):
            keys = slice(j * block, (j + 1) * block)
            scores = nt(k_s[g, keys, :], q) * factor - lse
            probs = jnp.where(offset <= limit - bases_ref[j], jnp.exp2(scores), 0.0)
            grad_soft = nt(v_s[g, keys, :], grad)
            grad_scores = (probs * (grad_soft - delta)).astype(BF16)
            dv_s[g, keys, :] += nn(probs.astype(BF16), grad)
            dk_s[g, keys, :] += nn(grad_scores, q)
            dqt = dqt + nn(kt_s[g, :, keys], grad_scores)
        results.append(dqt.T * scale)
    dq_ref[0] = turn(side_by_side(results, repeat, tile), cos_ref[...], sin_ref[...]).astype(BF16)

    @pl.when(pl.program_id(1) == pl.num_programs(1) - 1)
    def _():
        dkv_ref[0] = jnp.concatenate(
            [(dk_s[g] * scale).astype(BF16) for g in range(n_groups)]
            + [dv_s[g].astype(BF16) for g in range(n_groups)], axis=1)

def attend_back(query, kv_all, limits, lse, mixed, grad, cosine, sine, bases, tile=128):
    seqs, toks, q_width = query.shape
    length = kv_all.shape[1]
    n_groups = kv_all.shape[2] // (2 * HEAD_SIZE)
    repeat = q_width // HEAD_SIZE // n_groups
    n_blocks = bases.shape[0]
    block = length // n_blocks
    n_tiles = toks // tile
    rows = pl.BlockSpec((1, tile, q_width), lambda b, t, _: (b, t, 0))
    whole = pl.BlockSpec((1, length, kv_all.shape[2]), lambda b, t, _: (b, 0, 0))
    table = pl.BlockSpec((tile, q_width), lambda b, t, _: (t, 0))
    return pl.pallas_call(
        functools.partial(attend_back_kernel, n_groups, repeat, n_blocks, block),
        grid_spec=pltpu.PrefetchScalarGridSpec(
            num_scalar_prefetch=1,
            grid=(seqs, n_tiles),
            in_specs=[
                rows,
                whole,
                pl.BlockSpec((1, 1, 1, tile), lambda b, t, _: (b, t, 0, 0)),
                pl.BlockSpec((1, 1, n_groups, repeat * tile), lambda b, t, _: (b, t, 0, 0)),
                rows,
                rows,
                table,
                table,
            ],
            out_specs=[rows, whole],
            scratch_shapes=[
                pltpu.VMEM((n_groups, length, HEAD_SIZE), BF16),
                pltpu.VMEM((n_groups, length, HEAD_SIZE), BF16),
                pltpu.VMEM((n_groups, HEAD_SIZE, length), BF16),
                pltpu.VMEM((n_groups, length, HEAD_SIZE), F32),
                pltpu.VMEM((n_groups, length, HEAD_SIZE), F32),
            ],
        ),
        out_shape=[
            jax.ShapeDtypeStruct((seqs, toks, q_width), BF16),
            jax.ShapeDtypeStruct((seqs, length, kv_all.shape[2]), BF16),
        ],
        compiler_params=pltpu.CompilerParams(vmem_limit_bytes=VMEM_LIMIT),
        cost_estimate=pl.CostEstimate(
            flops=10 * seqs * toks * length * 256 * n_groups * repeat,
            bytes_accessed=8 * seqs * toks * q_width + 8 * seqs * length * q_width,
            transcendentals=seqs * toks * length * n_groups * repeat),
        name="attend_back",
    )(bases, query, kv_all, limits, lse, mixed, grad, cosine, sine)

def ffn_kernel(keep, steps, normed_ref, grad_ref, gate_ref, up_ref, down_ref, out_ref, back_ref, *rest):
    if steps > 1:
        out_acc, back_acc = rest[-2:]
    step = pl.program_id(1)
    normed = normed_ref[...]
    grad = grad_ref[...]
    gate_w, up_w, down_w = gate_ref[...], up_ref[...], down_ref[...]
    gate = nn(normed, gate_w)
    up = nn(normed, up_w)
    grad_hidden = nn(grad, down_w)
    sig = jax.nn.sigmoid(gate)
    silu = gate * sig
    hidden = (silu * up).astype(BF16)
    grad_gate = (grad_hidden * up * (sig + silu * (1.0 - sig))).astype(BF16)
    grad_up = (grad_hidden * silu).astype(BF16)
    if keep:
        for ref, value in zip(rest[:3], (hidden, grad_gate, grad_up)):
            ref[...] = value
    out_part = nt(hidden, down_w)
    back_part = nt(grad_gate, gate_w) + nt(grad_up, up_w)

    if steps == 1:
        out_ref[...] = out_part.astype(BF16)
        back_ref[...] = back_part.astype(BF16)
        return

    @pl.when(step == 0)
    def _():
        out_acc[...] = out_part
        back_acc[...] = back_part

    @pl.when(step > 0)
    def _():
        out_acc[...] += out_part
        back_acc[...] += back_part

    @pl.when(step == steps - 1)
    def _():
        out_ref[...] = out_acc[...].astype(BF16)
        back_ref[...] = back_acc[...].astype(BF16)

def ffn_slice(normed, grad, weights, keep, row_tile=256, tile=None):
    rows, width = normed.shape
    hidden = weights.shape[1] // 3
    tile = tile or hidden
    steps = hidden // tile
    row_spec = pl.BlockSpec((row_tile, width), lambda r, f: (r, 0))
    hid_spec = pl.BlockSpec((row_tile, tile), lambda r, f: (r, f))
    wide = jax.ShapeDtypeStruct((rows, width), BF16)
    hid = jax.ShapeDtypeStruct((rows, hidden), BF16)
    return pl.pallas_call(
        functools.partial(ffn_kernel, keep, steps),
        grid=(rows // row_tile, steps),
        in_specs=[
            row_spec,
            row_spec,
            pl.BlockSpec((width, tile), lambda r, f: (0, f)),
            pl.BlockSpec((width, tile), lambda r, f: (0, steps + f)),
            pl.BlockSpec((width, tile), lambda r, f: (0, 2 * steps + f)),
        ],
        out_specs=[row_spec, row_spec] + [hid_spec] * (3 if keep else 0),
        out_shape=[wide, wide] + [hid] * (3 if keep else 0),
        scratch_shapes=[pltpu.VMEM((row_tile, width), F32)] * (2 if steps > 1 else 0),
        compiler_params=pltpu.CompilerParams(vmem_limit_bytes=VMEM_LIMIT),
        cost_estimate=pl.CostEstimate(
            flops=12 * rows * width * hidden, bytes_accessed=8 * rows * width + 12 * width * hidden,
            transcendentals=rows * hidden),
        name="ffn_slice",
    )(normed, grad, weights, weights, weights)

def project_kernel(q_width, rows_ref, gain_ref, weight_ref, cos_ref, sin_ref, normed_ref, q_ref, kv_ref):
    rows = rows_ref[...].astype(F32)
    inverse = lax.rsqrt(jnp.mean(rows * rows, axis=-1, keepdims=True) + EPSILON)
    normed = (rows * inverse * gain_ref[...]).astype(BF16)
    normed_ref[...] = normed
    turned = turn(nn(normed, weight_ref[...]), cos_ref[...], sin_ref[...]).astype(BF16)
    q_ref[...] = turned[:, :q_width]
    kv_ref[...] = turned[:, q_width:]


def project(inputs, gain, weights, cosine, sine, q_width, row_tile=256):
    rows, width = inputs.shape
    out_width = cosine.shape[1]
    per_seq = cosine.shape[0] // row_tile
    table = pl.BlockSpec((row_tile, out_width), lambda r: (r % per_seq, 0))
    return pl.pallas_call(
        functools.partial(project_kernel, q_width),
        grid=(rows // row_tile,),
        in_specs=[
            pl.BlockSpec((row_tile, width), lambda r: (r, 0)),
            pl.BlockSpec((1, width), lambda r: (0, 0)),
            pl.BlockSpec((width, out_width), lambda r: (0, 0)),
            table,
            table,
        ],
        out_specs=[
            pl.BlockSpec((row_tile, width), lambda r: (r, 0)),
            pl.BlockSpec((row_tile, q_width), lambda r: (r, 0)),
            pl.BlockSpec((row_tile, out_width - q_width), lambda r: (r, 0)),
        ],
        out_shape=[
            jax.ShapeDtypeStruct((rows, width), BF16),
            jax.ShapeDtypeStruct((rows, q_width), BF16),
            jax.ShapeDtypeStruct((rows, out_width - q_width), BF16),
        ],
        compiler_params=pltpu.CompilerParams(vmem_limit_bytes=VMEM_LIMIT),
        cost_estimate=pl.CostEstimate(
            flops=2 * rows * width * out_width,
            bytes_accessed=4 * rows * width + 2 * width * out_width,
            transcendentals=rows,
        ),
        name="project",
    )(inputs, gain, weights, cosine, sine)


def sum_turn_kernel(count, cos_ref, sin_ref, *refs):
    total = refs[0][0].astype(F32)
    for ref in refs[1:count]:
        total = total + ref[0].astype(F32)
    refs[count][0] = turn(total, cos_ref[...], sin_ref[...]).astype(BF16)


def sum_turn(pieces, cosine, sine):
    toks, width = cosine.shape
    seqs = pieces[0].shape[0]
    block = pl.BlockSpec((1, toks, width), lambda b: (b, 0, 0))
    table = pl.BlockSpec((toks, width), lambda b: (0, 0))
    return pl.pallas_call(
        functools.partial(sum_turn_kernel, len(pieces)),
        grid=(seqs,),
        in_specs=[table, table] + [block] * len(pieces),
        out_specs=block,
        out_shape=jax.ShapeDtypeStruct((seqs, toks, width), BF16),
        compiler_params=pltpu.CompilerParams(vmem_limit_bytes=VMEM_LIMIT),
        name="sum_turn",
    )(cosine, sine, *pieces)


TILE = 128


def rotation_tables(positions, heads, plain):
    half_width = HEAD_SIZE // 2
    inverse = jnp.exp(
        jnp.arange(half_width, dtype=F32) * (-2.0 * math.log(ROPE_BASE) / HEAD_SIZE)
    )
    angles = positions.astype(F32)[:, None] * inverse[None, :]
    cosine, sine = jnp.cos(angles), jnp.sin(angles)
    still = jnp.ones((positions.shape[0], plain * HEAD_SIZE), F32)
    return (
        jnp.concatenate([cosine] * (2 * heads) + [still], axis=1),
        jnp.concatenate([-sine, sine] * heads + [0.0 * still], axis=1),
    )


def last_allowed(positions, start_row):
    begin = start_row[:, None, :]
    inside = (positions[None, :, None] >= begin) & (positions[None, :, None] < begin + PIECE)
    ends = jnp.where(inside, begin + PIECE - 1, -1)
    return jnp.maximum(positions[None, :], jnp.max(ends, axis=-1)).astype(jnp.int32)


def norm_back(grad_normed, hat_values, inverse_rms, gain_values):
    scaled = grad_normed * gain_values
    return inverse_rms * (
        scaled - hat_values * jnp.mean(scaled * hat_values, axis=-1, keepdims=True)
    )


def swap(value, axis, step):
    count = lax.axis_size(axis)
    return lax.ppermute(value, axis, [(i, i ^ step) for i in range(count)])


def partners(value, axis):
    return [value] + [swap(value, axis, j) for j in range(1, lax.axis_size(axis))]


def place(pieces, axis, dim):
    me = lax.axis_index(axis)
    width = pieces[0].shape[dim]
    shape = list(pieces[0].shape)
    shape[dim] = width * len(pieces)
    whole = jnp.zeros(shape, pieces[0].dtype)
    for j, piece in enumerate(pieces):
        whole = lax.dynamic_update_slice_in_dim(whole, piece, (me ^ j) * width, dim)
    return whole


def tn(left, right):
    return lax.dot_general(left, right, (((0,), (0,)), ((), ())), preferred_element_type=F32)


def local(
    inputs,
    starts,
    first_gain,
    query_weight,
    key_matrix,
    value_matrix,
    out_weight,
    second_gain,
    gate_weight,
    up_weight,
    down_weight,
    grad_out,
):
    seq_count, tok_count, model_width = inputs.shape
    q_width = query_weight.shape[1]
    kv_width = key_matrix.shape[1]
    local_heads = q_width // HEAD_SIZE
    group_heads = kv_width // HEAD_SIZE
    rows = seq_count * tok_count
    n_ctx = lax.axis_size("ctx")
    n_tp = lax.axis_size("tp")
    ctx = lax.axis_index("ctx")
    tp = lax.axis_index("tp")
    both = ("shard", "ctx")
    qkv_width = q_width + 2 * kv_width
    hidden = gate_weight.shape[1]

    own_rows = query_weight.shape[0]
    qkv_own = jnp.concatenate([query_weight, key_matrix, value_matrix], axis=1)
    gains_own = jnp.concatenate(
        [
            first_gain[:, None],
            second_gain[:, None],
            jnp.zeros((own_rows, LANES - 2), BF16),
        ],
        axis=1,
    )
    attn_own = jnp.concatenate([qkv_own, gains_own], axis=1)
    attn_full = place(partners(attn_own, "ctx"), "ctx", 0)
    attn_full = place(partners(attn_full, "shard"), "shard", 0)
    gain_one = attn_full[:, qkv_width].astype(F32)[None, :]
    gain_two = attn_full[:, qkv_width + 1].astype(F32)[None, :]

    ffn_own = jnp.concatenate([gate_weight, up_weight, down_weight.T], axis=1)
    ffn_slices = [
        lax.all_gather(piece, both, axis=0, tiled=True) for piece in partners(ffn_own, "tp")
    ]
    out_rows = place(partners(out_weight.T, "tp"), "tp", 1)
    out_full = lax.all_gather(out_rows, both, axis=0, tiled=True)
    qkv_rows = place(partners(qkv_own, "tp"), "tp", 1)
    qkv_full = lax.all_gather(qkv_rows, both, axis=0, tiled=True)

    query_pos = ctx * tok_count + jnp.arange(tok_count, dtype=jnp.int32)
    bases = jnp.stack([(ctx ^ j) * tok_count for j in range(n_ctx)]).astype(jnp.int32)
    limits = last_allowed(query_pos, starts).reshape(seq_count, tok_count // TILE, 1, TILE)
    cosine, sine = rotation_tables(query_pos, local_heads + group_heads, group_heads)
    rows_in = inputs.reshape(rows, model_width)
    normed_one, query_low, kv_own = project(
        rows_in, gain_one, attn_full, cosine, sine, q_width
    )
    query_low = query_low.reshape(seq_count, tok_count, q_width)
    kv_own = kv_own.reshape(seq_count, tok_count, 2 * kv_width)
    kv_all = jnp.concatenate(partners(kv_own, "ctx"), axis=1)
    mixed_seqs, lse = attend(query_low, kv_all, limits, bases, TILE)
    mixed_low = mixed_seqs.reshape(rows, q_width)
    mixed_all = place(partners(mixed_low, "tp"), "tp", 1)

    stream = rows_in.astype(F32)
    middle = stream + nt(mixed_all, out_full)
    inverse_two = lax.rsqrt(jnp.mean(middle * middle, axis=-1, keepdims=True) + EPSILON)
    hat_two = middle * inverse_two
    normed_two = (hat_two * gain_two).astype(BF16)
    grad_rows = grad_out.reshape(rows, model_width)

    total_out = middle
    grad_normed_two = jnp.zeros((rows, model_width), F32)
    for j in range(n_tp):
        out_term, back_term, *kept = ffn_slice(normed_two, grad_rows, ffn_slices[j], j == 0)
        total_out = total_out + out_term.astype(F32)
        grad_normed_two = grad_normed_two + back_term.astype(F32)
        if j == 0:
            hidden_low, grad_gate, grad_up = kept
            ffn_grads = jnp.concatenate(
                [
                    tn(normed_two, grad_gate).astype(BF16),
                    tn(normed_two, grad_up).astype(BF16),
                    tn(grad_rows, hidden_low).astype(BF16),
                ],
                axis=1,
            )
    ffn_grads = lax.psum_scatter(ffn_grads, both, scatter_dimension=0, tiled=True).astype(F32)
    result = total_out.astype(BF16).reshape(seq_count, tok_count, model_width)

    grad_gain_two = jnp.sum(grad_normed_two * hat_two, axis=0)
    grad_middle = grad_rows.astype(F32) + norm_back(grad_normed_two, hat_two, inverse_two, gain_two)
    grad_attn = grad_middle.astype(BF16)
    out_own = lax.dynamic_slice_in_dim(out_full, tp * q_width, q_width, 1)
    grad_out_rows = tn(grad_attn, mixed_low)
    grad_mixed = nn(grad_attn, out_own).astype(BF16).reshape(seq_count, tok_count, q_width)

    grad_query, grad_kv_all = attend_back(
        query_low,
        kv_all,
        limits,
        lse,
        mixed_seqs,
        grad_mixed,
        cosine[:, :q_width],
        -sine[:, :q_width],
        bases,
        TILE,
    )
    grad_query = grad_query.reshape(rows, q_width)
    pieces = [grad_kv_all] + [
        swap(grad_kv_all[:, j * tok_count : (j + 1) * tok_count], "ctx", j) for j in range(1, n_ctx)
    ]
    grad_kv = sum_turn(pieces, cosine[:, q_width:], -sine[:, q_width:]).reshape(rows, 2 * kv_width)
    grad_q_pieces = partners(grad_query, "tp")
    grad_kv_pieces = partners(grad_kv, "tp")
    grad_qkv_all = place(
        [jnp.concatenate(pair, axis=1) for pair in zip(grad_q_pieces, grad_kv_pieces)], "tp", 1
    )
    grad_normed_one = nt(grad_qkv_all, qkv_full)
    attn_grads = jnp.concatenate(
        [
            tn(normed_one, grad_query).astype(BF16),
            tn(normed_one, grad_kv).astype(BF16),
            grad_out_rows.astype(BF16),
            jnp.broadcast_to(grad_gain_two.astype(BF16)[:, None], (model_width, LANES)),
        ],
        axis=1,
    )
    attn_grads = lax.psum_scatter(attn_grads, both, scatter_dimension=0, tiled=True).astype(F32)

    inverse_one = lax.rsqrt(jnp.mean(stream * stream, axis=-1, keepdims=True) + EPSILON)
    hat_one = stream * inverse_one
    grad_gain_one = jnp.sum(grad_normed_one * hat_one, axis=0)
    for axis in both:
        pieces = partners(grad_gain_one, axis)
        grad_gain_one = sum(pieces[1:], pieces[0])
    part = lax.axis_index("shard") * n_ctx + ctx
    grad_gain_one = lax.dynamic_slice_in_dim(grad_gain_one, part * own_rows, own_rows, 0)
    grad_stream = grad_middle + norm_back(grad_normed_one, hat_one, inverse_one, gain_one)
    grad_inputs = grad_stream.astype(BF16).reshape(seq_count, tok_count, model_width)
    return (
        result,
        grad_inputs,
        grad_gain_one,
        attn_grads[:, :q_width],
        attn_grads[:, q_width : q_width + kv_width],
        attn_grads[:, q_width + kv_width : qkv_width],
        attn_grads[:, qkv_width : qkv_width + q_width].T,
        attn_grads[:, qkv_width + q_width],
        ffn_grads[:, :hidden],
        ffn_grads[:, hidden : 2 * hidden],
        ffn_grads[:, 2 * hidden :].T,
    )


def solution(mesh):
    both = ("shard", "ctx")
    rows = P("shard", "ctx", None)
    return jax.shard_map(
        local,
        mesh=mesh,
        in_specs=(
            rows,
            P("shard", None),
            P(both),
            P(both, "tp"),
            P(both, "tp"),
            P(both, "tp"),
            P("tp", both),
            P(both),
            P(both, "tp"),
            P(both, "tp"),
            P("tp", both),
            rows,
        ),
        out_specs=(
            rows,
            rows,
            P(both),
            P(both, "tp"),
            P(both, "tp"),
            P(both, "tp"),
            P("tp", both),
            P(both),
            P(both, "tp"),
            P(both, "tp"),
            P("tp", both),
        ),
        check_vma=False,
    )
```

```python
import functools
import math

import jax
import jax.numpy as jnp
from jax import lax
from jax.experimental import pallas as pl
from jax.experimental.pallas import tpu as pltpu
from jax.sharding import PartitionSpec as P

HEAD_SIZE = 96
PIECE = 256

EPSILON = 1e-05
ROPE_BASE = 100000.0
NEGATIVE = -1e30
F32 = jnp.float32
BF16 = jnp.bfloat16
LANES = 128
VMEM_LIMIT = 56 << 20
COST_SCALE = 3


def nt(left, right):
    return lax.dot_general(left, right, (((1,), (1,)), ((), ())), preferred_element_type=F32)


def nn(left, right):
    return jnp.dot(left, right, preferred_element_type=F32)


def params():
    return pltpu.CompilerParams(vmem_limit_bytes=VMEM_LIMIT)


def cost(flops, bytes_accessed, transcendentals=0):
    return pl.CostEstimate(
        flops=int(flops * COST_SCALE),
        bytes_accessed=int(bytes_accessed * COST_SCALE),
        transcendentals=int(transcendentals * COST_SCALE),
    )


def columns(array, start, size):
    if size % LANES or start % size:
        array, start = array[:, start : start + size], 0
    return array, pl.BlockSpec((array.shape[0], size), lambda r: (0, start // size))


def turn(value, cosine, sine):
    half = HEAD_SIZE // 2
    width = value.shape[-1]
    lane = lax.broadcasted_iota(jnp.int32, (1, width), 1) % HEAD_SIZE
    other = jnp.where(
        jnp.broadcast_to(lane, value.shape) < half, pltpu.roll(value, width - half, 1), pltpu.roll(value, half, 1)
    )
    return value * cosine + other * sine


def project_kernel(q_width, rows_ref, gain_ref, weight_ref, cos_ref, sin_ref, normed_ref, q_ref, kv_ref):
    rows = rows_ref[...].astype(F32)
    inverse = lax.rsqrt(jnp.mean(rows * rows, axis=-1, keepdims=True) + EPSILON)
    normed = (rows * inverse * gain_ref[...]).astype(BF16)
    normed_ref[...] = normed
    turned = turn(nn(normed, weight_ref[...]), cos_ref[...], sin_ref[...]).astype(BF16)
    q_ref[...] = turned[:, :q_width]
    kv_ref[...] = turned[:, q_width:]


def project(inputs, gain, weights, cosine, sine, q_width, row_tile=256):
    rows, width = inputs.shape
    out_width = cosine.shape[1]
    per_seq = cosine.shape[0] // row_tile
    table = pl.BlockSpec((row_tile, out_width), lambda r: (r % per_seq, 0))
    return pl.pallas_call(
        functools.partial(project_kernel, q_width),
        grid=(rows // row_tile,),
        in_specs=[
            pl.BlockSpec((row_tile, width), lambda r: (r, 0)),
            pl.BlockSpec((1, width), lambda r: (0, 0)),
            pl.BlockSpec((width, out_width), lambda r: (0, 0)),
            table,
            table,
        ],
        out_specs=[
            pl.BlockSpec((row_tile, width), lambda r: (r, 0)),
            pl.BlockSpec((row_tile, q_width), lambda r: (r, 0)),
            pl.BlockSpec((row_tile, out_width - q_width), lambda r: (r, 0)),
        ],
        out_shape=[
            jax.ShapeDtypeStruct((rows, width), BF16),
            jax.ShapeDtypeStruct((rows, q_width), BF16),
            jax.ShapeDtypeStruct((rows, out_width - q_width), BF16),
        ],
        compiler_params=params(),
        cost_estimate=cost(2 * rows * width * out_width, 4 * rows * width + 2 * width * out_width),
        name="project",
    )(inputs, gain, weights, cosine, sine)


def stacked(block, group, repeat):
    first = group * repeat
    return jnp.concatenate(
        [
            block[:, (first + r) * HEAD_SIZE : (first + r + 1) * HEAD_SIZE]
            for r in range(repeat)
        ],
        axis=0,
    )


def side_by_side(groups, repeat, tile):
    return jnp.concatenate(
        [g[r * tile : (r + 1) * tile] for g in groups for r in range(repeat)], axis=1
    )


def attend_kernel(n_groups, repeat, n_blocks, bases_ref, q_ref, limit_ref, *refs):
    kv_refs = refs[:n_blocks]
    mixed_ref, lse_ref, k_s, vt_s = refs[n_blocks:]
    tile = q_ref.shape[0]
    block = kv_refs[0].shape[0]
    cols = repeat * tile
    kv_width = n_groups * HEAD_SIZE
    factor = HEAD_SIZE ** (-0.5) * math.log2(math.e)

    @pl.when(pl.program_id(0) == 0)
    def _():
        for j, ref in enumerate(kv_refs):
            for g in range(n_groups):
                first = g * HEAD_SIZE
                k_s[g, j] = ref[:, first : first + HEAD_SIZE]
                vt_s[g, j] = ref[:, kv_width + first : kv_width + first + HEAD_SIZE].T

    limit = jnp.concatenate([limit_ref[0, 0]] * repeat, axis=1)
    offset = lax.broadcasted_iota(jnp.int32, (block, cols), 0)
    results = []
    for g in range(n_groups):
        q = stacked(q_ref[...], g, repeat)
        blocks = []
        for j in range(n_blocks):
            scores = nt(k_s[g, j], q) * factor
            blocks.append(jnp.where(offset <= limit - bases_ref[j], scores, NEGATIVE))
        top = functools.reduce(
            jnp.maximum, [jnp.max(x, axis=0, keepdims=True) for x in blocks]
        )
        total = jnp.zeros((1, cols), F32)
        acc = jnp.zeros((HEAD_SIZE, cols), F32)
        for j in range(n_blocks):
            probs = jnp.exp2(blocks[j] - top)
            total = total + jnp.sum(probs, axis=0, keepdims=True)
            acc = acc + nn(vt_s[g, j], probs.astype(BF16))
        lse_ref[0, g : g + 1, :] = top + jnp.log2(total)
        results.append((acc / total).T)
    mixed_ref[...] = side_by_side(results, repeat, tile).astype(BF16)


def attend(query, kv_pieces, limits, bases, seq):
    _, toks, q_width = query.shape
    n_blocks = len(kv_pieces)
    block, kv_cols = toks, kv_pieces[0].shape[1]
    n_groups = kv_cols // (2 * HEAD_SIZE)
    repeat = q_width // HEAD_SIZE // n_groups
    n_tiles = toks // TILE
    length = block * n_blocks
    return pl.pallas_call(
        functools.partial(attend_kernel, n_groups, repeat, n_blocks),
        grid_spec=pltpu.PrefetchScalarGridSpec(
            num_scalar_prefetch=1,
            grid=(n_tiles,),
            in_specs=[
                pl.BlockSpec((None, TILE, q_width), lambda t, _: (seq, t, 0)),
                pl.BlockSpec((1, 1, 1, TILE), lambda t, _: (seq, t, 0, 0)),
            ]
            + [pl.BlockSpec((block, kv_cols), lambda t, _: (seq, 0))] * n_blocks,
            out_specs=[
                pl.BlockSpec((TILE, q_width), lambda t, _: (t, 0)),
                pl.BlockSpec((1, n_groups, repeat * TILE), lambda t, _: (t, 0, 0)),
            ],
            scratch_shapes=[
                pltpu.VMEM((n_groups, n_blocks, block, HEAD_SIZE), BF16),
                pltpu.VMEM((n_groups, n_blocks, HEAD_SIZE, block), BF16),
            ],
        ),
        out_shape=[
            jax.ShapeDtypeStruct((toks, q_width), BF16),
            jax.ShapeDtypeStruct((n_tiles, n_groups, repeat * TILE), F32),
        ],
        compiler_params=params(),
        cost_estimate=cost(
            4 * toks * length * 256 * n_groups * repeat,
            4 * toks * q_width + 2 * length * kv_cols,
            toks * length * n_groups * repeat,
        ),
        name="attend",
    )(bases, query, limits, *kv_pieces)


def attend_back_kernel(n_groups, repeat, n_blocks, bases_ref, q_ref, limit_ref, lse_ref, mixed_ref, grad_ref, cos_ref, sin_ref, *refs):
    kv_refs, refs = refs[:n_blocks], refs[n_blocks:]
    dq_ref, dkv_ref, k_s, v_s, kt_s, dk_s, dv_s = refs
    tile = q_ref.shape[0]
    block = kv_refs[0].shape[0]
    cols = repeat * tile
    kv_width = n_groups * HEAD_SIZE
    scale = HEAD_SIZE ** (-0.5)
    factor = scale * math.log2(math.e)

    @pl.when(pl.program_id(0) == 0)
    def _():
        for j, ref in enumerate(kv_refs):
            for g in range(n_groups):
                first = g * HEAD_SIZE
                k = ref[:, first : first + HEAD_SIZE]
                k_s[g, j] = k
                kt_s[g, j] = k.T
                v_s[g, j] = ref[:, kv_width + first : kv_width + first + HEAD_SIZE]
        dk_s[...] = jnp.zeros_like(dk_s)
        dv_s[...] = jnp.zeros_like(dv_s)

    limit = jnp.concatenate([limit_ref[0, 0]] * repeat, axis=1)
    offset = lax.broadcasted_iota(jnp.int32, (block, cols), 0)
    ones = jnp.ones((8, HEAD_SIZE), BF16)
    results = []
    for g in range(n_groups):
        q = stacked(q_ref[...], g, repeat)
        grad = stacked(grad_ref[...], g, repeat)
        mixed = stacked(mixed_ref[...], g, repeat)
        product = grad.astype(F32) * mixed.astype(F32)
        high = product.astype(BF16)
        low = (product - high.astype(F32)).astype(BF16)
        delta = (nt(ones, high) + nt(ones, low))[0:1]
        lse = lse_ref[0, g : g + 1, :]
        dqt = jnp.zeros((HEAD_SIZE, cols), F32)
        for j in range(n_blocks):
            scores = nt(k_s[g, j], q) * factor - lse
            probs = jnp.where(offset <= limit - bases_ref[j], jnp.exp2(scores), 0.0)
            grad_soft = nt(v_s[g, j], grad)
            grad_scores = (probs * (grad_soft - delta)).astype(BF16)
            dv_s[g, j] += nn(probs.astype(BF16), grad)
            dk_s[g, j] += nn(grad_scores, q)
            dqt = dqt + nn(kt_s[g, j], grad_scores)
        results.append(dqt.T * scale)
    dq_ref[...] = turn(side_by_side(results, repeat, tile), cos_ref[...], -sin_ref[...]).astype(BF16)

    @pl.when(pl.program_id(0) == pl.num_programs(0) - 1)
    def _():
        for j in range(n_blocks):
            rows = pl.ds(pl.multiple_of(bases_ref[j], block), block)
            dkv_ref[rows, :] = jnp.concatenate(
                [(dk_s[g, j] * scale).astype(BF16) for g in range(n_groups)]
                + [dv_s[g, j].astype(BF16) for g in range(n_groups)],
                axis=1,
            )


def attend_back(query, kv_pieces, limits, lse, mixed, grad, cosine, sine, bases, seq):
    _, toks, q_width = query.shape
    n_blocks = len(kv_pieces)
    block, kv_cols = toks, kv_pieces[0].shape[1]
    n_groups = kv_cols // (2 * HEAD_SIZE)
    repeat = q_width // HEAD_SIZE // n_groups
    n_tiles = toks // TILE
    length = block * n_blocks
    rows = pl.BlockSpec((TILE, q_width), lambda t, _: (t, 0))
    kv_piece = pl.BlockSpec((block, kv_cols), lambda t, _: (seq, 0))
    return pl.pallas_call(
        functools.partial(attend_back_kernel, n_groups, repeat, n_blocks),
        grid_spec=pltpu.PrefetchScalarGridSpec(
            num_scalar_prefetch=1,
            grid=(n_tiles,),
            in_specs=[
                pl.BlockSpec((None, TILE, q_width), lambda t, _: (seq, t, 0)),
                pl.BlockSpec((1, 1, 1, TILE), lambda t, _: (seq, t, 0, 0)),
                pl.BlockSpec((1, n_groups, repeat * TILE), lambda t, _: (t, 0, 0)),
                rows,
                rows,
                rows,
                rows,
            ]
            + [kv_piece] * n_blocks,
            out_specs=[rows, pl.BlockSpec((length, kv_cols), lambda t, _: (0, 0))],
            scratch_shapes=[
                pltpu.VMEM((n_groups, n_blocks, block, HEAD_SIZE), BF16),
                pltpu.VMEM((n_groups, n_blocks, block, HEAD_SIZE), BF16),
                pltpu.VMEM((n_groups, n_blocks, HEAD_SIZE, block), BF16),
                pltpu.VMEM((n_groups, n_blocks, block, HEAD_SIZE), F32),
                pltpu.VMEM((n_groups, n_blocks, block, HEAD_SIZE), F32),
            ],
        ),
        out_shape=[
            jax.ShapeDtypeStruct((toks, q_width), BF16),
            jax.ShapeDtypeStruct((length, kv_cols), BF16),
        ],
        compiler_params=params(),
        cost_estimate=cost(
            10 * toks * length * 256 * n_groups * repeat,
            8 * toks * q_width + 4 * length * kv_cols,
            toks * length * n_groups * repeat,
        ),
        name="attend_back",
    )(bases, query, limits, lse, mixed, grad, cosine, sine, *kv_pieces)


def project_back_kernel(query_ref, cos_ref, sin_ref, weight_ref, terms_ref, kv_ref, part_ref):
    total = jnp.sum(terms_ref[...].astype(F32), axis=0)
    kv = turn(total, cos_ref[...], -sin_ref[...]).astype(BF16)
    kv_ref[...] = kv
    both = jnp.concatenate([query_ref[...], kv], axis=1)
    part_ref[...] = nt(both, weight_ref[...]).astype(BF16)


def project_back(query, terms, cosine, sine, weights):
    toks, kv_cols = cosine.shape
    count = terms.shape[0] // toks
    width, columns = weights.shape[0], query.shape[1] + kv_cols

    def whole(rows, cols):
        return pl.BlockSpec((rows, cols), lambda r: (0, 0))

    return pl.pallas_call(
        project_back_kernel,
        grid=(1,),
        in_specs=[
            whole(*query.shape),
            whole(toks, kv_cols),
            whole(toks, kv_cols),
            whole(width, columns),
            pl.BlockSpec((count, toks, kv_cols), lambda r: (0, 0, 0)),
        ],
        out_specs=[whole(toks, kv_cols), whole(toks, width)],
        out_shape=[
            jax.ShapeDtypeStruct((toks, kv_cols), BF16),
            jax.ShapeDtypeStruct((toks, width), BF16),
        ],
        compiler_params=params(),
        cost_estimate=cost(2 * toks * width * columns, 2 * width * (toks + columns)),
        name="project_back",
    )(query, cosine, sine, weights, terms.reshape(count, toks, kv_cols))


def middle_kernel(count, rows_ref, gain_ref, weight_ref, *refs):
    middle_ref, normed_ref = refs[count:]
    mixed = jnp.concatenate([ref[...] for ref in refs[:count]], axis=1)
    middle = rows_ref[...].astype(F32) + nt(mixed, weight_ref[...])
    inverse = lax.rsqrt(jnp.mean(middle * middle, axis=-1, keepdims=True) + EPSILON)
    middle_ref[...] = middle
    normed_ref[...] = (middle * inverse * gain_ref[...]).astype(BF16)


def middle_of(inputs, gain, weights, start, pieces, seq, row_tile=256):
    width = inputs.shape[1]
    toks, q_width = pieces[0].shape
    steps = toks // row_tile
    rows = pl.BlockSpec((row_tile, width), lambda r: (r, 0))
    weights, weight_spec = columns(weights, start, q_width * len(pieces))
    return pl.pallas_call(
        functools.partial(middle_kernel, len(pieces)),
        grid=(steps,),
        in_specs=[
            pl.BlockSpec((row_tile, width), lambda r: (seq * steps + r, 0)),
            pl.BlockSpec((1, width), lambda r: (0, 0)),
            weight_spec,
        ]
        + [pl.BlockSpec((row_tile, q_width), lambda r: (r, 0))] * len(pieces),
        out_specs=[rows, rows],
        out_shape=[
            jax.ShapeDtypeStruct((toks, width), F32),
            jax.ShapeDtypeStruct((toks, width), BF16),
        ],
        compiler_params=params(),
        cost_estimate=cost(
            2 * toks * width * width, 10 * toks * width + 2 * width * width
        ),
        name="middle_of",
    )(inputs, gain, weights, *pieces)


def ffn_kernel(keep, based, groups, normed_ref, grad_ref, *refs):
    weight_refs, refs = refs[: 3 * groups], refs[3 * groups :]
    normed, grad = normed_ref[...], grad_ref[...]
    out = back = None
    if based:
        out, back = refs[0][...].astype(F32), refs[1][...].astype(F32)
        refs = refs[2:]
    for g in range(groups):
        gate_w, up_w, down_w = [ref[...] for ref in weight_refs[3 * g : 3 * g + 3]]
        gate = nn(normed, gate_w)
        up = nn(normed, up_w)
        grad_hidden = nn(grad, down_w)
        sig = jax.nn.sigmoid(gate)
        silu = gate * sig
        hidden = (silu * up).astype(BF16)
        grad_gate = (grad_hidden * up * (sig + silu * (1.0 - sig))).astype(BF16)
        grad_up = (grad_hidden * silu).astype(BF16)
        out_g = nt(hidden, down_w)
        back_g = nt(grad_gate, gate_w) + nt(grad_up, up_w)
        out = out_g if out is None else out + out_g
        back = back_g if back is None else back + back_g
        if keep and g == 0:
            refs[2][...] = jnp.concatenate([grad_gate, grad_up, hidden], axis=1)
    refs[0][...] = out.astype(BF16)
    refs[1][...] = back.astype(BF16)


def ffn_groups(normed, grad, weights, hidden, seq, base, keep, row_tile=256):
    toks, width = normed.shape
    steps = toks // row_tile
    groups = len(weights)
    rows = pl.BlockSpec((row_tile, width), lambda r: (r, 0))
    kept = pl.BlockSpec((row_tile, 3 * hidden), lambda r: (r, 0))
    wide = jax.ShapeDtypeStruct((toks, width), BF16)
    return pl.pallas_call(
        functools.partial(ffn_kernel, keep, bool(base), groups),
        grid=(steps,),
        in_specs=[rows, pl.BlockSpec((row_tile, width), lambda r: (seq * steps + r, 0))]
        + [
            pl.BlockSpec((width, hidden), lambda r, c=c: (0, c), pipeline_mode=pl.Buffered(1))
            for _ in weights
            for c in range(3)
        ]
        + [rows] * len(base),
        out_specs=[rows, rows] + [kept] * int(keep),
        out_shape=[wide, wide] + [jax.ShapeDtypeStruct((toks, 3 * hidden), BF16)] * int(keep),
        compiler_params=params(),
        cost_estimate=cost(
            12 * groups * toks * width * hidden,
            8 * toks * width + 6 * groups * width * hidden,
            groups * toks * hidden,
        ),
        name="ffn_groups",
    )(normed, grad, *[w for w in weights for _ in range(3)], *base)


def grad_middle_kernel(count, middle_ref, grad_ref, gain_ref, weight_ref, *refs):
    wide_ref, attn_ref, mixed_ref, gain_grad_ref = refs[count:]
    middle = middle_ref[...]
    inverse = lax.rsqrt(jnp.mean(middle * middle, axis=-1, keepdims=True) + EPSILON)
    hat = middle * inverse
    back = refs[0][...].astype(F32)
    for ref in refs[1:count]:
        back = back + ref[...].astype(F32)
    scaled = back * gain_ref[...]
    total = grad_ref[...].astype(F32) + inverse * (
        scaled - hat * jnp.mean(scaled * hat, axis=-1, keepdims=True)
    )
    wide_ref[...] = total
    attn = total.astype(BF16)
    attn_ref[...] = attn
    mixed_ref[...] = nn(attn, weight_ref[...]).astype(BF16)
    part = jnp.sum(back * hat, axis=0, keepdims=True)

    @pl.when(pl.program_id(0) == 0)
    def _():
        gain_grad_ref[...] = part

    @pl.when(pl.program_id(0) > 0)
    def _():
        gain_grad_ref[...] += part


def grad_middle_of(middle, grad, gain, weights, start, backs, q_width, seq, row_tile=256):
    toks, width = middle.shape
    steps = toks // row_tile
    rows = pl.BlockSpec((row_tile, width), lambda r: (r, 0))
    line = pl.BlockSpec((1, width), lambda r: (0, 0))
    weights, weight = columns(weights, start, q_width)
    return pl.pallas_call(
        functools.partial(grad_middle_kernel, len(backs)),
        grid=(steps,),
        in_specs=[
            rows,
            pl.BlockSpec((row_tile, width), lambda r: (seq * steps + r, 0)),
            line,
            weight,
        ]
        + [rows] * len(backs),
        out_specs=[rows, rows, pl.BlockSpec((row_tile, q_width), lambda r: (r, 0)), line],
        out_shape=[
            jax.ShapeDtypeStruct((toks, width), F32),
            jax.ShapeDtypeStruct((toks, width), BF16),
            jax.ShapeDtypeStruct((toks, q_width), BF16),
            jax.ShapeDtypeStruct((1, width), F32),
        ],
        compiler_params=params(),
        cost_estimate=cost(2 * toks * width * q_width, 16 * toks * width),
        name="grad_middle_of",
    )(middle, grad, gain, weights, *backs)


def weight_grad_kernel(n_seqs, tile, split, *refs):
    lefts, others, rights = refs[:n_seqs], refs[n_seqs : 2 * n_seqs], refs[2 * n_seqs : 3 * n_seqs]
    out_ref, left_s, other_s = refs[3 * n_seqs :]
    toks = lefts[0].shape[0]

    @pl.when(pl.program_id(0) == 0)
    def _():
        for s in range(n_seqs):
            left_s[:, s * toks : (s + 1) * toks] = lefts[s][...].T
            other_s[:, s * toks : (s + 1) * toks] = others[s][...].T

    right = jnp.concatenate([ref[...] for ref in rights], axis=0)
    if split % tile:
        out_ref[...] = jnp.concatenate(
            [nn(left_s[...], right[:, :split]), nn(other_s[...], right[:, split:])], axis=1
        ).astype(BF16)
        return
    first = pl.program_id(0) < split // tile

    @pl.when(first)
    def _():
        out_ref[...] = nn(left_s[...], right).astype(BF16)

    @pl.when(jnp.logical_not(first))
    def _():
        out_ref[...] = nn(other_s[...], right).astype(BF16)


def weight_grad(lefts, others, rights, split, tile):
    toks, width = lefts[0].shape
    columns = rights[0].shape[1]
    if tile % LANES or columns % tile or split % tile:
        tile = columns
    n_seqs = len(lefts)
    whole = pl.BlockSpec((toks, width), lambda c: (0, 0))
    return pl.pallas_call(
        functools.partial(weight_grad_kernel, n_seqs, tile, split),
        grid=(columns // tile,),
        in_specs=[whole] * (2 * n_seqs)
        + [pl.BlockSpec((toks, tile), lambda c: (0, c))] * n_seqs,
        out_specs=pl.BlockSpec((width, tile), lambda c: (0, c)),
        out_shape=jax.ShapeDtypeStruct((width, columns), BF16),
        scratch_shapes=[pltpu.VMEM((width, n_seqs * toks), BF16)] * 2,
        compiler_params=params(),
        cost_estimate=cost(
            2 * n_seqs * toks * width * columns,
            2 * n_seqs * toks * (2 * width + columns) + 2 * width * columns,
        ),
        name="weight_grad",
    )(*lefts, *others, *rights)


def grad_inputs_kernel(rows_ref, wide_ref, gain_ref, terms_ref, out_ref, gain_grad_ref):
    rows = rows_ref[...].astype(F32)
    inverse = lax.rsqrt(jnp.mean(rows * rows, axis=-1, keepdims=True) + EPSILON)
    hat = rows * inverse
    back = jnp.sum(terms_ref[...].astype(F32), axis=0)
    scaled = back * gain_ref[...]
    total = wide_ref[...] + inverse * (
        scaled - hat * jnp.mean(scaled * hat, axis=-1, keepdims=True)
    )
    out_ref[...] = total.astype(BF16)
    gain_grad_ref[...] = jnp.sum(back * hat, axis=0, keepdims=True)


def grad_inputs_of(inputs, wide, gain, terms):
    toks, width = inputs.shape
    return pl.pallas_call(
        grad_inputs_kernel,
        out_shape=[
            jax.ShapeDtypeStruct((toks, width), BF16),
            jax.ShapeDtypeStruct((1, width), F32),
        ],
        compiler_params=params(),
        cost_estimate=cost(0, 16 * toks * width),
        name="grad_inputs_of",
    )(inputs, wide, gain, terms.reshape(-1, toks, width))


TILE = 128


def rotation_tables(positions, turned, plain):
    half = HEAD_SIZE // 2
    lane = jnp.arange((turned + plain) * HEAD_SIZE, dtype=jnp.int32)
    inverse = jnp.exp(
        (lane % half).astype(F32) * (-2.0 * math.log(ROPE_BASE) / HEAD_SIZE)
    )
    turns = lane < turned * HEAD_SIZE
    angles = positions.astype(F32)[:, None] * inverse[None, :]
    sign = jnp.where(turns, jnp.where(lane % HEAD_SIZE < half, -1.0, 1.0), 0.0)
    return jnp.where(turns, jnp.cos(angles), 1.0), jnp.sin(angles) * sign


def last_allowed(positions, start_row):
    begin = start_row[:, None, :]
    inside = (positions[None, :, None] >= begin) & (positions[None, :, None] < begin + PIECE)
    ends = jnp.where(inside, begin + PIECE - 1, -1)
    return jnp.maximum(positions[None, :], jnp.max(ends, axis=-1)).astype(jnp.int32)


def swap(value, axis, step):
    count = lax.axis_size(axis)
    return lax.ppermute(value, axis, [(i, i ^ step) for i in range(count)])


def partners(value, axis):
    return [value] + [swap(value, axis, j) for j in range(1, lax.axis_size(axis))]


def place(pieces, axis, dim):
    me = lax.axis_index(axis)
    width = pieces[0].shape[dim]
    shape = list(pieces[0].shape)
    shape[dim] = width * len(pieces)
    whole = jnp.zeros(shape, pieces[0].dtype)
    for j, piece in enumerate(pieces):
        whole = lax.dynamic_update_slice_in_dim(whole, piece, (me ^ j) * width, dim)
    return whole


def after(value, *others):
    return lax.optimization_barrier((value, *others))[0]


def sum_over(value, axis):
    pieces = partners(value, axis)
    return sum(pieces[1:], pieces[0])


def local(
    inputs,
    starts,
    first_gain,
    query_weight,
    key_matrix,
    value_matrix,
    out_weight,
    second_gain,
    gate_weight,
    up_weight,
    down_weight,
    grad_out,
):
    n_seqs, toks, width = inputs.shape
    q_width = query_weight.shape[1]
    kv_width = key_matrix.shape[1]
    qkv_width = q_width + 2 * kv_width
    turned = (q_width + kv_width) // HEAD_SIZE
    own_rows = query_weight.shape[0]
    hidden = gate_weight.shape[1]
    n_ctx = lax.axis_size("ctx")
    n_tp = lax.axis_size("tp")
    ctx = lax.axis_index("ctx")
    tp = lax.axis_index("tp")
    both = ("shard", "ctx")
    seqs = range(n_seqs)
    block = toks // n_tp

    def gather(value):
        return lax.all_gather(value, both, axis=0, tiled=True)

    last = []

    def step(kernel, first, *rest, **kwargs):
        out = kernel(after(first, *last) if last else first, *rest, **kwargs)
        last[:] = [out[0] if isinstance(out, (list, tuple)) else out]
        return out

    gains_own = jnp.concatenate(
        [
            first_gain[:, None],
            second_gain[:, None],
            jnp.zeros((own_rows, LANES - 2), BF16),
        ],
        axis=1,
    )
    qkv_own = jnp.concatenate([query_weight, key_matrix, value_matrix], axis=1)
    attn_own = jnp.concatenate([qkv_own, gains_own], axis=1)
    query_pos = ctx * toks + jnp.arange(toks, dtype=jnp.int32)
    bases = jnp.stack([(ctx ^ j) * toks for j in range(n_ctx)]).astype(jnp.int32)
    limits = last_allowed(query_pos, starts).reshape(n_seqs, toks // TILE, 1, TILE)
    cosine, sine = rotation_tables(query_pos, turned, kv_width // HEAD_SIZE)
    attn_pieces = partners(attn_own, "ctx")
    out_pieces = partners(out_weight.T, "tp")
    attn_part = place(attn_pieces, "ctx", 0)
    attn_part, cosine, sine, *out_pieces = lax.optimization_barrier(
        (attn_part, cosine, sine, *out_pieces)
    )
    attn_full = place(partners(attn_part, "shard"), "shard", 0)
    gain_one = attn_full[:, qkv_width].astype(F32)[None, :]
    gain_two = attn_full[:, qkv_width + 1].astype(F32)[None, :]

    ffn_own = jnp.concatenate([gate_weight, up_weight, down_weight.T], axis=1)
    own_full = gather(jnp.concatenate([ffn_own, *out_pieces], axis=1))
    out_start = 3 * hidden
    ffn_far = [swap(after(ffn_own, *attn_pieces), "tp", j) for j in range(2, n_tp, 2)]

    rows_in = inputs.reshape(n_seqs * toks, width)
    grad_rows = grad_out.reshape(n_seqs * toks, width)
    normed_one, query_low, kv_own = step(
        project, rows_in, gain_one, attn_full, cosine, sine, q_width
    )
    query_low = query_low.reshape(n_seqs, toks, q_width)

    kv_pieces = partners(kv_own, "ctx")
    mixed, lse, mixed_all = [], [], []
    ffn_weights = [own_full]
    for s in seqs:
        mixed_s, lse_s = step(attend, query_low, kv_pieces, limits, bases, s)
        mixed.append(mixed_s)
        lse.append(lse_s)
        mixed_all.append(partners(mixed_s, "tp"))
        if s == 0:
            ffn_weights += [gather(after(far, mixed_s)) for far in ffn_far]

    middle, normed_two, out_terms, backs, kept = [], [], [], [], []
    for s in seqs:
        middle_s, normed_s = step(middle_of, rows_in, gain_two, own_full, out_start, mixed_all[s], s)
        terms = ()
        batches = [ffn_weights] if s else [ffn_weights[:1]] + [[w] for w in ffn_weights[1:]]
        for j, weights in enumerate(batches):
            terms = step(ffn_groups, normed_s, grad_rows, weights, hidden, s, terms, j == 0)
            if j == 0:
                kept.append(terms[2])
                terms = terms[:2]
        middle.append(middle_s)
        normed_two.append(normed_s)
        out_terms.append(terms[0])
        backs.append([terms[1]] + ([swap(terms[1], "tp", 1)] if n_tp > 1 else []))
    out_near = jnp.concatenate(out_terms, axis=0)

    grad_wide, grad_attn, grad_query, grad_kv, gain_two_parts = [], [], [], [], []
    grad_pieces, gain_one_parts = [], []
    q_cos, q_sin = cosine[:, :q_width], sine[:, :q_width]
    kv_cos, kv_sin = cosine[:, q_width:], sine[:, q_width:]

    def through_attention(s):
        wide_s, attn_s, grad_mixed, gain_s = step(
            grad_middle_of, middle[s], grad_rows, gain_two, own_full, out_start, backs[s], q_width, s
        )
        query_s, kv_terms = step(
            attend_back,
            query_low,
            kv_pieces,
            limits,
            lse[s],
            mixed[s],
            grad_mixed,
            q_cos,
            q_sin,
            bases,
            s,
        )
        grad_wide.append(wide_s)
        grad_attn.append(attn_s)
        gain_two_parts.append(gain_s)
        grad_query.append(query_s)
        return lax.all_to_all(kv_terms, "ctx", 0, 0, tiled=True)

    def to_owners(s, parts):
        kv_s, part_s = step(project_back, grad_query[s], parts, kv_cos, kv_sin, attn_full)
        grad_kv.append(kv_s)
        return lax.all_to_all(part_s, "tp", 0, 0, tiled=True)

    def through_norm(s, pieces):
        rows_s = lax.dynamic_slice_in_dim(rows_in, s * toks + tp * block, block, 0)
        wide_s = lax.dynamic_slice_in_dim(grad_wide[s], tp * block, block, 0)
        grad_s, gain_s = step(grad_inputs_of, rows_s, wide_s, gain_one, pieces)
        gain_one_parts.append(gain_s)
        grad_pieces.append(partners(grad_s, "tp"))

    ffn_grads, out_far, pieces = None, out_near, []
    for s in seqs:
        parts = through_attention(s)
        if s == 0:
            if n_tp > 1:
                out_far = swap(after(out_near, grad_query[0]), "tp", 1)
            rights = [after(kept[0], *last), *kept[1:]]
            ffn_grads = weight_grad(
                normed_two,
                [grad_rows[i * toks : (i + 1) * toks] for i in seqs],
                rights,
                2 * hidden,
                256,
            )
            last[:] = [ffn_grads]
            ffn_grads = lax.psum_scatter(ffn_grads, both, scatter_dimension=0, tiled=True)
        else:
            through_norm(s - 1, pieces)
            parts = after(parts, out_far)
        pieces = to_owners(s, parts)
    grad_attn[0] = after(grad_attn[0], ffn_grads, *last)
    attn_grads = weight_grad(
        [normed_one[s * toks : (s + 1) * toks] for s in seqs],
        grad_attn,
        [jnp.concatenate([grad_query[s], grad_kv[s], mixed[s]], axis=1) for s in seqs],
        qkv_width,
        384,
    )
    last[:] = [attn_grads]
    attn_grads = lax.psum_scatter(attn_grads, both, scatter_dimension=0, tiled=True).astype(F32)
    through_norm(n_seqs - 1, pieces)
    grads = [place(pieces, "tp", 0) for pieces in grad_pieces]
    gain_one_parts[0] = after(gain_one_parts[0], grad_pieces[-1][min(1, n_tp - 1)])

    total = jnp.concatenate(middle, axis=0) + out_near.astype(F32)
    if n_tp > 1:
        total = total + out_far.astype(F32)
    result = total.astype(BF16).reshape(n_seqs, toks, width)

    gain_grads = jnp.concatenate(
        [sum_over(sum(gain_one_parts), "tp"), sum(gain_two_parts)], axis=0
    )
    for axis in both:
        gain_grads = sum_over(gain_grads, axis)
    part = lax.axis_index("shard") * n_ctx + ctx
    gain_grads = lax.dynamic_slice_in_dim(gain_grads, part * own_rows, own_rows, 1)
    return (
        result,
        jnp.stack(grads),
        gain_grads[0],
        attn_grads[:, :q_width],
        attn_grads[:, q_width : q_width + kv_width],
        attn_grads[:, q_width + kv_width : qkv_width],
        attn_grads[:, qkv_width:].T,
        gain_grads[1],
        ffn_grads[:, :hidden].astype(F32),
        ffn_grads[:, hidden : 2 * hidden].astype(F32),
        ffn_grads[:, 2 * hidden :].T.astype(F32),
    )


def solution(mesh):
    both = ("shard", "ctx")
    rows = P("shard", "ctx", None)
    return jax.shard_map(
        local,
        mesh=mesh,
        in_specs=(
            rows,
            P("shard", None),
            P(both),
            P(both, "tp"),
            P(both, "tp"),
            P(both, "tp"),
            P("tp", both),
            P(both),
            P(both, "tp"),
            P(both, "tp"),
            P("tp", both),
            rows,
        ),
        out_specs=(
            rows,
            rows,
            P(both),
            P(both, "tp"),
            P(both, "tp"),
            P(both, "tp"),
            P("tp", both),
            P(both),
            P(both, "tp"),
            P(both, "tp"),
            P("tp", both),
        ),
        check_vma=False,
    )
```

```python
import functools
import math

import jax
import jax.numpy as jnp
from jax import lax
from jax.experimental import pallas as pl
from jax.experimental.pallas import tpu as pltpu
from jax.sharding import PartitionSpec as P

HEAD_SIZE = 96
PIECE = 256

EPSILON = 1e-05
ROPE_BASE = 100000.0
NEGATIVE = -1e30
F32 = jnp.float32
BF16 = jnp.bfloat16
LANES = 128
VMEM_LIMIT = 56 << 20
TAIL = 30.0
COST_SCALE = 10


def nt(left, right):
    return lax.dot_general(left, right, (((1,), (1,)), ((), ())), preferred_element_type=F32)


def nn(left, right):
    return jnp.dot(left, right, preferred_element_type=F32)


def params():
    return pltpu.CompilerParams(vmem_limit_bytes=VMEM_LIMIT)


def cost(flops, bytes_accessed, transcendentals=0, weight=1.0):
    return pl.CostEstimate(
        flops=int(flops * COST_SCALE * weight),
        bytes_accessed=int(bytes_accessed * COST_SCALE * weight),
        transcendentals=int(transcendentals * COST_SCALE * weight),
    )


def tail_cost(*args, **kwargs):
    return cost(*args, **kwargs, weight=TAIL)


def columns(array, start, size):
    if size % LANES or start % size:
        array, start = array[:, start : start + size], 0
    return array, pl.BlockSpec((array.shape[0], size), lambda r: (0, start // size))


def turn(value, cosine, sine):
    half = HEAD_SIZE // 2
    width = value.shape[-1]
    lane = lax.broadcasted_iota(jnp.int32, (1, width), 1) % HEAD_SIZE
    other = jnp.where(
        jnp.broadcast_to(lane, value.shape) < half, pltpu.roll(value, width - half, 1), pltpu.roll(value, half, 1)
    )
    return value * cosine + other * sine


def project_kernel(q_width, rows_ref, gain_ref, weight_ref, cos_ref, sin_ref, normed_ref, q_ref, kv_ref):
    rows = rows_ref[...].astype(F32)
    inverse = lax.rsqrt(jnp.mean(rows * rows, axis=-1, keepdims=True) + EPSILON)
    normed = (rows * inverse * gain_ref[...]).astype(BF16)
    normed_ref[...] = normed
    turned = turn(nn(normed, weight_ref[...]), cos_ref[...], sin_ref[...]).astype(BF16)
    q_ref[...] = turned[:, :q_width]
    kv_ref[...] = turned[:, q_width:]


def project(inputs, gain, weights, cosine, sine, q_width, row_tile=256):
    rows, width = inputs.shape
    out_width = cosine.shape[1]
    per_seq = cosine.shape[0] // row_tile
    table = pl.BlockSpec((row_tile, out_width), lambda r: (r % per_seq, 0))
    return pl.pallas_call(
        functools.partial(project_kernel, q_width),
        grid=(rows // row_tile,),
        in_specs=[
            pl.BlockSpec((row_tile, width), lambda r: (r, 0)),
            pl.BlockSpec((1, width), lambda r: (0, 0)),
            pl.BlockSpec((width, out_width), lambda r: (0, 0)),
            table,
            table,
        ],
        out_specs=[
            pl.BlockSpec((row_tile, width), lambda r: (r, 0)),
            pl.BlockSpec((row_tile, q_width), lambda r: (r, 0)),
            pl.BlockSpec((row_tile, out_width - q_width), lambda r: (r, 0)),
        ],
        out_shape=[
            jax.ShapeDtypeStruct((rows, width), BF16),
            jax.ShapeDtypeStruct((rows, q_width), BF16),
            jax.ShapeDtypeStruct((rows, out_width - q_width), BF16),
        ],
        compiler_params=params(),
        cost_estimate=cost(2 * rows * width * out_width, 4 * rows * width + 2 * width * out_width),
        name="project",
    )(inputs, gain, weights, cosine, sine)


def stacked(block, group, repeat):
    first = group * repeat
    return jnp.concatenate(
        [
            block[:, (first + r) * HEAD_SIZE : (first + r + 1) * HEAD_SIZE]
            for r in range(repeat)
        ],
        axis=0,
    )


def side_by_side(groups, repeat, tile):
    return jnp.concatenate(
        [g[r * tile : (r + 1) * tile] for g in groups for r in range(repeat)], axis=1
    )


def attend_kernel(n_groups, repeat, n_blocks, bases_ref, q_ref, limit_ref, *refs):
    kv_refs = refs[:n_blocks]
    mixed_ref, lse_ref, k_s, vt_s = refs[n_blocks:]
    tile = q_ref.shape[0]
    block = kv_refs[0].shape[0]
    cols = repeat * tile
    kv_width = n_groups * HEAD_SIZE
    factor = HEAD_SIZE ** (-0.5) * math.log2(math.e)

    @pl.when(pl.program_id(0) == 0)
    def _():
        for j, ref in enumerate(kv_refs):
            for g in range(n_groups):
                first = g * HEAD_SIZE
                k_s[g, j] = ref[:, first : first + HEAD_SIZE]
                vt_s[g, j] = ref[:, kv_width + first : kv_width + first + HEAD_SIZE].T

    limit = jnp.concatenate([limit_ref[0, 0]] * repeat, axis=1)
    offset = lax.broadcasted_iota(jnp.int32, (block, cols), 0)
    results = []
    for g in range(n_groups):
        q = stacked(q_ref[...], g, repeat)
        blocks = []
        for j in range(n_blocks):
            scores = nt(k_s[g, j], q) * factor
            blocks.append(jnp.where(offset <= limit - bases_ref[j], scores, NEGATIVE))
        top = functools.reduce(
            jnp.maximum, [jnp.max(x, axis=0, keepdims=True) for x in blocks]
        )
        total = jnp.zeros((1, cols), F32)
        acc = jnp.zeros((HEAD_SIZE, cols), F32)
        for j in range(n_blocks):
            probs = jnp.exp2(blocks[j] - top)
            total = total + jnp.sum(probs, axis=0, keepdims=True)
            acc = acc + nn(vt_s[g, j], probs.astype(BF16))
        lse_ref[0, g : g + 1, :] = top + jnp.log2(total)
        results.append((acc / total).T)
    mixed_ref[...] = side_by_side(results, repeat, tile).astype(BF16)


def attend(query, kv_pieces, limits, bases, seq):
    _, toks, q_width = query.shape
    n_blocks = len(kv_pieces)
    block, kv_cols = toks, kv_pieces[0].shape[1]
    n_groups = kv_cols // (2 * HEAD_SIZE)
    repeat = q_width // HEAD_SIZE // n_groups
    n_tiles = toks // TILE
    length = block * n_blocks
    return pl.pallas_call(
        functools.partial(attend_kernel, n_groups, repeat, n_blocks),
        grid_spec=pltpu.PrefetchScalarGridSpec(
            num_scalar_prefetch=1,
            grid=(n_tiles,),
            in_specs=[
                pl.BlockSpec((None, TILE, q_width), lambda t, _: (seq, t, 0)),
                pl.BlockSpec((1, 1, 1, TILE), lambda t, _: (seq, t, 0, 0)),
            ]
            + [pl.BlockSpec((block, kv_cols), lambda t, _: (seq, 0))] * n_blocks,
            out_specs=[
                pl.BlockSpec((TILE, q_width), lambda t, _: (t, 0)),
                pl.BlockSpec((1, n_groups, repeat * TILE), lambda t, _: (t, 0, 0)),
            ],
            scratch_shapes=[
                pltpu.VMEM((n_groups, n_blocks, block, HEAD_SIZE), BF16),
                pltpu.VMEM((n_groups, n_blocks, HEAD_SIZE, block), BF16),
            ],
        ),
        out_shape=[
            jax.ShapeDtypeStruct((toks, q_width), BF16),
            jax.ShapeDtypeStruct((n_tiles, n_groups, repeat * TILE), F32),
        ],
        compiler_params=params(),
        cost_estimate=cost(
            4 * toks * length * 256 * n_groups * repeat,
            4 * toks * q_width + 2 * length * kv_cols,
            toks * length * n_groups * repeat,
        ),
        name="attend",
    )(bases, query, limits, *kv_pieces)


def attend_back_kernel(n_groups, repeat, n_blocks, bases_ref, q_ref, limit_ref, lse_ref, mixed_ref, grad_ref, cos_ref, sin_ref, *refs):
    kv_refs, refs = refs[:n_blocks], refs[n_blocks:]
    dq_ref, dkv_ref, k_s, v_s, kt_s, dk_s, dv_s = refs
    tile = q_ref.shape[0]
    block = kv_refs[0].shape[0]
    cols = repeat * tile
    kv_width = n_groups * HEAD_SIZE
    scale = HEAD_SIZE ** (-0.5)
    factor = scale * math.log2(math.e)

    @pl.when(pl.program_id(0) == 0)
    def _():
        for j, ref in enumerate(kv_refs):
            for g in range(n_groups):
                first = g * HEAD_SIZE
                k = ref[:, first : first + HEAD_SIZE]
                k_s[g, j] = k
                kt_s[g, j] = k.T
                v_s[g, j] = ref[:, kv_width + first : kv_width + first + HEAD_SIZE]
        dk_s[...] = jnp.zeros_like(dk_s)
        dv_s[...] = jnp.zeros_like(dv_s)

    limit = jnp.concatenate([limit_ref[0, 0]] * repeat, axis=1)
    offset = lax.broadcasted_iota(jnp.int32, (block, cols), 0)
    ones = jnp.ones((8, HEAD_SIZE), BF16)
    results = []
    for g in range(n_groups):
        q = stacked(q_ref[...], g, repeat)
        grad = stacked(grad_ref[...], g, repeat)
        mixed = stacked(mixed_ref[...], g, repeat)
        product = grad.astype(F32) * mixed.astype(F32)
        high = product.astype(BF16)
        low = (product - high.astype(F32)).astype(BF16)
        delta = (nt(ones, high) + nt(ones, low))[0:1]
        lse = lse_ref[0, g : g + 1, :]
        dqt = jnp.zeros((HEAD_SIZE, cols), F32)
        for j in range(n_blocks):
            scores = nt(k_s[g, j], q) * factor - lse
            probs = jnp.where(offset <= limit - bases_ref[j], jnp.exp2(scores), 0.0)
            grad_soft = nt(v_s[g, j], grad)
            grad_scores = (probs * (grad_soft - delta)).astype(BF16)
            dv_s[g, j] += nn(probs.astype(BF16), grad)
            dk_s[g, j] += nn(grad_scores, q)
            dqt = dqt + nn(kt_s[g, j], grad_scores)
        results.append(dqt.T * scale)
    dq_ref[...] = turn(side_by_side(results, repeat, tile), cos_ref[...], -sin_ref[...]).astype(BF16)

    @pl.when(pl.program_id(0) == pl.num_programs(0) - 1)
    def _():
        for j in range(n_blocks):
            rows = pl.ds(pl.multiple_of(bases_ref[j], block), block)
            dkv_ref[rows, :] = jnp.concatenate(
                [(dk_s[g, j] * scale).astype(BF16) for g in range(n_groups)]
                + [dv_s[g, j].astype(BF16) for g in range(n_groups)],
                axis=1,
            )


def attend_back(query, kv_pieces, limits, lse, mixed, grad, cosine, sine, bases, seq):
    _, toks, q_width = query.shape
    n_blocks = len(kv_pieces)
    block, kv_cols = toks, kv_pieces[0].shape[1]
    n_groups = kv_cols // (2 * HEAD_SIZE)
    repeat = q_width // HEAD_SIZE // n_groups
    n_tiles = toks // TILE
    length = block * n_blocks
    rows = pl.BlockSpec((TILE, q_width), lambda t, _: (t, 0))
    kv_piece = pl.BlockSpec((block, kv_cols), lambda t, _: (seq, 0))
    return pl.pallas_call(
        functools.partial(attend_back_kernel, n_groups, repeat, n_blocks),
        grid_spec=pltpu.PrefetchScalarGridSpec(
            num_scalar_prefetch=1,
            grid=(n_tiles,),
            in_specs=[
                pl.BlockSpec((None, TILE, q_width), lambda t, _: (seq, t, 0)),
                pl.BlockSpec((1, 1, 1, TILE), lambda t, _: (seq, t, 0, 0)),
                pl.BlockSpec((1, n_groups, repeat * TILE), lambda t, _: (t, 0, 0)),
                rows,
                rows,
                rows,
                rows,
            ]
            + [kv_piece] * n_blocks,
            out_specs=[rows, pl.BlockSpec((length, kv_cols), lambda t, _: (0, 0))],
            scratch_shapes=[
                pltpu.VMEM((n_groups, n_blocks, block, HEAD_SIZE), BF16),
                pltpu.VMEM((n_groups, n_blocks, block, HEAD_SIZE), BF16),
                pltpu.VMEM((n_groups, n_blocks, HEAD_SIZE, block), BF16),
                pltpu.VMEM((n_groups, n_blocks, block, HEAD_SIZE), F32),
                pltpu.VMEM((n_groups, n_blocks, block, HEAD_SIZE), F32),
            ],
        ),
        out_shape=[
            jax.ShapeDtypeStruct((toks, q_width), BF16),
            jax.ShapeDtypeStruct((length, kv_cols), BF16),
        ],
        compiler_params=params(),
        cost_estimate=tail_cost(
            10 * toks * length * 256 * n_groups * repeat,
            8 * toks * q_width + 4 * length * kv_cols,
            toks * length * n_groups * repeat,
        ),
        name="attend_back",
    )(bases, query, limits, lse, mixed, grad, cosine, sine, *kv_pieces)


def project_back_kernel(query_ref, cos_ref, sin_ref, weight_ref, terms_ref, kv_ref, part_ref):
    total = jnp.sum(terms_ref[...].astype(F32), axis=0)
    kv = turn(total, cos_ref[...], -sin_ref[...]).astype(BF16)
    kv_ref[...] = kv
    both = jnp.concatenate([query_ref[...], kv], axis=1)
    part_ref[...] = nt(both, weight_ref[...]).astype(BF16)


def project_back(query, terms, cosine, sine, weights):
    toks, kv_cols = cosine.shape
    count = terms.shape[0] // toks
    width, columns = weights.shape[0], query.shape[1] + kv_cols

    def whole(rows, cols):
        return pl.BlockSpec((rows, cols), lambda r: (0, 0))

    return pl.pallas_call(
        project_back_kernel,
        grid=(1,),
        in_specs=[
            whole(*query.shape),
            whole(toks, kv_cols),
            whole(toks, kv_cols),
            whole(width, columns),
            pl.BlockSpec((count, toks, kv_cols), lambda r: (0, 0, 0)),
        ],
        out_specs=[whole(toks, kv_cols), whole(toks, width)],
        out_shape=[
            jax.ShapeDtypeStruct((toks, kv_cols), BF16),
            jax.ShapeDtypeStruct((toks, width), BF16),
        ],
        compiler_params=params(),
        cost_estimate=tail_cost(
            2 * toks * width * columns, 2 * width * (toks + columns)
        ),
        name="project_back",
    )(query, cosine, sine, weights, terms.reshape(count, toks, kv_cols))


def middle_kernel(count, rows_ref, gain_ref, weight_ref, *refs):
    middle_ref, normed_ref = refs[count:]
    mixed = jnp.concatenate([ref[...] for ref in refs[:count]], axis=1)
    middle = rows_ref[...].astype(F32) + nt(mixed, weight_ref[...])
    inverse = lax.rsqrt(jnp.mean(middle * middle, axis=-1, keepdims=True) + EPSILON)
    middle_ref[...] = middle
    normed_ref[...] = (middle * inverse * gain_ref[...]).astype(BF16)


def middle_of(inputs, gain, weights, start, pieces, seq, row_tile=256):
    width = inputs.shape[1]
    toks, q_width = pieces[0].shape
    steps = toks // row_tile
    rows = pl.BlockSpec((row_tile, width), lambda r: (r, 0))
    weights, weight_spec = columns(weights, start, q_width * len(pieces))
    return pl.pallas_call(
        functools.partial(middle_kernel, len(pieces)),
        grid=(steps,),
        in_specs=[
            pl.BlockSpec((row_tile, width), lambda r: (seq * steps + r, 0)),
            pl.BlockSpec((1, width), lambda r: (0, 0)),
            weight_spec,
        ]
        + [pl.BlockSpec((row_tile, q_width), lambda r: (r, 0))] * len(pieces),
        out_specs=[rows, rows],
        out_shape=[
            jax.ShapeDtypeStruct((toks, width), F32),
            jax.ShapeDtypeStruct((toks, width), BF16),
        ],
        compiler_params=params(),
        cost_estimate=cost(
            2 * toks * width * width, 10 * toks * width + 2 * width * width
        ),
        name="middle_of",
    )(inputs, gain, weights, *pieces)


def ffn_kernel(keep, based, groups, normed_ref, grad_ref, *refs):
    weight_refs, refs = refs[: 3 * groups], refs[3 * groups :]
    normed, grad = normed_ref[...], grad_ref[...]
    out = back = None
    if based:
        out, back = refs[0][...].astype(F32), refs[1][...].astype(F32)
        refs = refs[2:]
    for g in range(groups):
        gate_w, up_w, down_w = [ref[...] for ref in weight_refs[3 * g : 3 * g + 3]]
        gate = nn(normed, gate_w)
        up = nn(normed, up_w)
        grad_hidden = nn(grad, down_w)
        sig = jax.nn.sigmoid(gate)
        silu = gate * sig
        hidden = (silu * up).astype(BF16)
        grad_gate = (grad_hidden * up * (sig + silu * (1.0 - sig))).astype(BF16)
        grad_up = (grad_hidden * silu).astype(BF16)
        out_g = nt(hidden, down_w)
        back_g = nt(grad_gate, gate_w) + nt(grad_up, up_w)
        out = out_g if out is None else out + out_g
        back = back_g if back is None else back + back_g
        if keep and g == 0:
            refs[2][...] = jnp.concatenate([grad_gate, grad_up, hidden], axis=1)
    refs[0][...] = out.astype(BF16)
    refs[1][...] = back.astype(BF16)


def ffn_groups(normed, grad, weights, hidden, seq, base, keep, row_tile=256):
    toks, width = normed.shape
    steps = toks // row_tile
    groups = len(weights)
    rows = pl.BlockSpec((row_tile, width), lambda r: (r, 0))
    kept = pl.BlockSpec((row_tile, 3 * hidden), lambda r: (r, 0))
    wide = jax.ShapeDtypeStruct((toks, width), BF16)
    return pl.pallas_call(
        functools.partial(ffn_kernel, keep, bool(base), groups),
        grid=(steps,),
        in_specs=[rows, pl.BlockSpec((row_tile, width), lambda r: (seq * steps + r, 0))]
        + [
            pl.BlockSpec((width, hidden), lambda r, c=c: (0, c), pipeline_mode=pl.Buffered(1))
            for _ in weights
            for c in range(3)
        ]
        + [rows] * len(base),
        out_specs=[rows, rows] + [kept] * int(keep),
        out_shape=[wide, wide] + [jax.ShapeDtypeStruct((toks, 3 * hidden), BF16)] * int(keep),
        compiler_params=params(),
        cost_estimate=cost(
            12 * groups * toks * width * hidden,
            8 * toks * width + 6 * groups * width * hidden,
            groups * toks * hidden,
        ),
        name="ffn_groups",
    )(normed, grad, *[w for w in weights for _ in range(3)], *base)


def grad_middle_kernel(count, middle_ref, grad_ref, gain_ref, weight_ref, *refs):
    wide_ref, attn_ref, mixed_ref, gain_grad_ref = refs[count:]
    middle = middle_ref[...]
    inverse = lax.rsqrt(jnp.mean(middle * middle, axis=-1, keepdims=True) + EPSILON)
    hat = middle * inverse
    back = refs[0][...].astype(F32)
    for ref in refs[1:count]:
        back = back + ref[...].astype(F32)
    scaled = back * gain_ref[...]
    total = grad_ref[...].astype(F32) + inverse * (
        scaled - hat * jnp.mean(scaled * hat, axis=-1, keepdims=True)
    )
    wide_ref[...] = total
    attn = total.astype(BF16)
    attn_ref[...] = attn
    mixed_ref[...] = nn(attn, weight_ref[...]).astype(BF16)
    part = jnp.sum(back * hat, axis=0, keepdims=True)

    @pl.when(pl.program_id(0) == 0)
    def _():
        gain_grad_ref[...] = part

    @pl.when(pl.program_id(0) > 0)
    def _():
        gain_grad_ref[...] += part


def grad_middle_of(middle, grad, gain, weights, start, backs, q_width, seq, row_tile=256):
    toks, width = middle.shape
    steps = toks // row_tile
    rows = pl.BlockSpec((row_tile, width), lambda r: (r, 0))
    line = pl.BlockSpec((1, width), lambda r: (0, 0))
    weights, weight = columns(weights, start, q_width)
    return pl.pallas_call(
        functools.partial(grad_middle_kernel, len(backs)),
        grid=(steps,),
        in_specs=[
            rows,
            pl.BlockSpec((row_tile, width), lambda r: (seq * steps + r, 0)),
            line,
            weight,
        ]
        + [rows] * len(backs),
        out_specs=[rows, rows, pl.BlockSpec((row_tile, q_width), lambda r: (r, 0)), line],
        out_shape=[
            jax.ShapeDtypeStruct((toks, width), F32),
            jax.ShapeDtypeStruct((toks, width), BF16),
            jax.ShapeDtypeStruct((toks, q_width), BF16),
            jax.ShapeDtypeStruct((1, width), F32),
        ],
        compiler_params=params(),
        cost_estimate=tail_cost(2 * toks * width * q_width, 16 * toks * width),
        name="grad_middle_of",
    )(middle, grad, gain, weights, *backs)


def weight_grad_kernel(n_seqs, tile, split, *refs):
    lefts, others, rights = refs[:n_seqs], refs[n_seqs : 2 * n_seqs], refs[2 * n_seqs : 3 * n_seqs]
    out_ref, left_s, other_s = refs[3 * n_seqs :]
    toks = lefts[0].shape[0]

    @pl.when(pl.program_id(0) == 0)
    def _():
        for s in range(n_seqs):
            left_s[:, s * toks : (s + 1) * toks] = lefts[s][...].T
            other_s[:, s * toks : (s + 1) * toks] = others[s][...].T

    right = jnp.concatenate([ref[...] for ref in rights], axis=0)
    if split % tile:
        out_ref[...] = jnp.concatenate(
            [nn(left_s[...], right[:, :split]), nn(other_s[...], right[:, split:])], axis=1
        ).astype(BF16)
        return
    first = pl.program_id(0) < split // tile

    @pl.when(first)
    def _():
        out_ref[...] = nn(left_s[...], right).astype(BF16)

    @pl.when(jnp.logical_not(first))
    def _():
        out_ref[...] = nn(other_s[...], right).astype(BF16)


def weight_grad(lefts, others, rights, split, tile):
    toks, width = lefts[0].shape
    columns = rights[0].shape[1]
    if tile % LANES or columns % tile or split % tile:
        tile = columns
    n_seqs = len(lefts)
    whole = pl.BlockSpec((toks, width), lambda c: (0, 0))
    return pl.pallas_call(
        functools.partial(weight_grad_kernel, n_seqs, tile, split),
        grid=(columns // tile,),
        in_specs=[whole] * (2 * n_seqs)
        + [pl.BlockSpec((toks, tile), lambda c: (0, c))] * n_seqs,
        out_specs=pl.BlockSpec((width, tile), lambda c: (0, c)),
        out_shape=jax.ShapeDtypeStruct((width, columns), BF16),
        scratch_shapes=[pltpu.VMEM((width, n_seqs * toks), BF16)] * 2,
        compiler_params=params(),
        cost_estimate=tail_cost(
            2 * n_seqs * toks * width * columns,
            2 * n_seqs * toks * (2 * width + columns) + 2 * width * columns,
        ),
        name="weight_grad",
    )(*lefts, *others, *rights)


def grad_inputs_kernel(rows_ref, wide_ref, gain_ref, *refs):
    *term_refs, out_ref, gain_grad_ref = refs
    rows = rows_ref[...].astype(F32)
    inverse = lax.rsqrt(jnp.mean(rows * rows, axis=-1, keepdims=True) + EPSILON)
    hat = rows * inverse
    back = term_refs[0][...].astype(F32)
    for ref in term_refs[1:]:
        back = back + ref[...].astype(F32)
    scaled = back * gain_ref[...]
    total = wide_ref[...] + inverse * (
        scaled - hat * jnp.mean(scaled * hat, axis=-1, keepdims=True)
    )
    out_ref[...] = total.astype(BF16)
    gain_grad_ref[...] = jnp.sum(back * hat, axis=0, keepdims=True)


def grad_inputs_of(inputs, wide, gain, terms):
    toks, width = inputs.shape
    return pl.pallas_call(
        grad_inputs_kernel,
        out_shape=[
            jax.ShapeDtypeStruct((toks, width), BF16),
            jax.ShapeDtypeStruct((1, width), F32),
        ],
        compiler_params=params(),
        cost_estimate=tail_cost(0, 16 * toks * width),
        name="grad_inputs_of",
    )(inputs, wide, gain, *terms)


TILE = 128


def rotation_tables(positions, turned, plain):
    half = HEAD_SIZE // 2
    lane = jnp.arange((turned + plain) * HEAD_SIZE, dtype=jnp.int32)
    inverse = jnp.exp(
        (lane % half).astype(F32) * (-2.0 * math.log(ROPE_BASE) / HEAD_SIZE)
    )
    turns = lane < turned * HEAD_SIZE
    angles = positions.astype(F32)[:, None] * inverse[None, :]
    sign = jnp.where(turns, jnp.where(lane % HEAD_SIZE < half, -1.0, 1.0), 0.0)
    return jnp.where(turns, jnp.cos(angles), 1.0), jnp.sin(angles) * sign


def last_allowed(positions, start_row):
    begin = start_row[:, None, :]
    inside = (positions[None, :, None] >= begin) & (positions[None, :, None] < begin + PIECE)
    ends = jnp.where(inside, begin + PIECE - 1, -1)
    return jnp.maximum(positions[None, :], jnp.max(ends, axis=-1)).astype(jnp.int32)


def swap(value, axis, step):
    count = lax.axis_size(axis)
    return lax.ppermute(value, axis, [(i, i ^ step) for i in range(count)])


def partners(value, axis):
    return [value] + [swap(value, axis, j) for j in range(1, lax.axis_size(axis))]


def place(pieces, axis, dim):
    me = lax.axis_index(axis)
    width = pieces[0].shape[dim]
    shape = list(pieces[0].shape)
    shape[dim] = width * len(pieces)
    whole = jnp.zeros(shape, pieces[0].dtype)
    for j, piece in enumerate(pieces):
        whole = lax.dynamic_update_slice_in_dim(whole, piece, (me ^ j) * width, dim)
    return whole


def exchange(value, axis):
    me = lax.axis_index(axis)
    count = lax.axis_size(axis)
    size = value.shape[0] // count
    blocks = [lax.dynamic_slice_in_dim(value, (me ^ j) * size, size, 0) for j in range(count)]
    return [blocks[0]] + [swap(blocks[j], axis, j) for j in range(1, count)]


def after(value, *others):
    return lax.optimization_barrier((value, *others))[0]


def sum_over(value, axis):
    pieces = partners(value, axis)
    return sum(pieces[1:], pieces[0])


def local(
    inputs,
    starts,
    first_gain,
    query_weight,
    key_matrix,
    value_matrix,
    out_weight,
    second_gain,
    gate_weight,
    up_weight,
    down_weight,
    grad_out,
):
    n_seqs, toks, width = inputs.shape
    q_width = query_weight.shape[1]
    kv_width = key_matrix.shape[1]
    qkv_width = q_width + 2 * kv_width
    turned = (q_width + kv_width) // HEAD_SIZE
    own_rows = query_weight.shape[0]
    hidden = gate_weight.shape[1]
    n_ctx = lax.axis_size("ctx")
    n_tp = lax.axis_size("tp")
    ctx = lax.axis_index("ctx")
    tp = lax.axis_index("tp")
    both = ("shard", "ctx")
    seqs = range(n_seqs)
    block = toks // n_tp

    def gather(value):
        return lax.all_gather(value, both, axis=0, tiled=True)

    last = []

    def step(kernel, first, *rest, **kwargs):
        out = kernel(after(first, *last) if last else first, *rest, **kwargs)
        last[:] = [out[0] if isinstance(out, (list, tuple)) else out]
        return out

    gains_own = jnp.concatenate(
        [
            first_gain[:, None],
            second_gain[:, None],
            jnp.zeros((own_rows, LANES - 2), BF16),
        ],
        axis=1,
    )
    qkv_own = jnp.concatenate([query_weight, key_matrix, value_matrix], axis=1)
    attn_own = jnp.concatenate([qkv_own, gains_own], axis=1)
    query_pos = ctx * toks + jnp.arange(toks, dtype=jnp.int32)
    bases = jnp.stack([(ctx ^ j) * toks for j in range(n_ctx)]).astype(jnp.int32)
    limits = last_allowed(query_pos, starts).reshape(n_seqs, toks // TILE, 1, TILE)
    cosine, sine = rotation_tables(query_pos, turned, kv_width // HEAD_SIZE)
    attn_pieces = partners(attn_own, "ctx")
    out_pieces = partners(out_weight.T, "tp")
    attn_part = place(attn_pieces, "ctx", 0)
    attn_part, cosine, sine, *out_pieces = lax.optimization_barrier(
        (attn_part, cosine, sine, *out_pieces)
    )
    attn_full = place(partners(attn_part, "shard"), "shard", 0)
    gain_one = attn_full[:, qkv_width].astype(F32)[None, :]
    gain_two = attn_full[:, qkv_width + 1].astype(F32)[None, :]

    ffn_own = jnp.concatenate([gate_weight, up_weight, down_weight.T], axis=1)
    own_full = gather(jnp.concatenate([ffn_own, *out_pieces], axis=1))
    out_start = 3 * hidden
    ffn_far = [swap(after(ffn_own, *attn_pieces), "tp", j) for j in range(2, n_tp, 2)]

    rows_in = inputs.reshape(n_seqs * toks, width)
    grad_rows = grad_out.reshape(n_seqs * toks, width)
    normed_one, query_low, kv_own = step(
        project, rows_in, gain_one, attn_full, cosine, sine, q_width
    )
    query_low = query_low.reshape(n_seqs, toks, q_width)

    kv_pieces = partners(kv_own, "ctx")
    mixed, lse, mixed_all = [], [], []
    ffn_weights = [own_full]
    for s in seqs:
        mixed_s, lse_s = step(attend, query_low, kv_pieces, limits, bases, s)
        mixed.append(mixed_s)
        lse.append(lse_s)
        mixed_all.append(partners(mixed_s, "tp"))
        if s == 0:
            ffn_weights += [gather(after(far, mixed_s)) for far in ffn_far]

    middle, normed_two, out_terms, backs, kept = [], [], [], [], []
    for s in seqs:
        middle_s, normed_s = step(middle_of, rows_in, gain_two, own_full, out_start, mixed_all[s], s)
        terms = ()
        batches = [ffn_weights] if s else [ffn_weights[:1]] + [[w] for w in ffn_weights[1:]]
        for j, weights in enumerate(batches):
            terms = step(ffn_groups, normed_s, grad_rows, weights, hidden, s, terms, j == 0)
            if j == 0:
                kept.append(terms[2])
                terms = terms[:2]
        middle.append(middle_s)
        normed_two.append(normed_s)
        out_terms.append(terms[0])
        backs.append([terms[1]] + ([swap(terms[1], "tp", 1)] if n_tp > 1 else []))
    out_near = jnp.concatenate(out_terms, axis=0)

    grad_wide, grad_attn, grad_query, grad_kv, gain_two_parts = [], [], [], [], []
    grad_pieces, gain_one_parts = [], []
    q_cos, q_sin = cosine[:, :q_width], sine[:, :q_width]
    kv_cos, kv_sin = cosine[:, q_width:], sine[:, q_width:]

    def through_middle(s):
        wide_s, attn_s, grad_mixed, gain_s = step(
            grad_middle_of, middle[s], grad_rows, gain_two, own_full, out_start, backs[s], q_width, s
        )
        grad_wide.append(wide_s)
        grad_attn.append(attn_s)
        gain_two_parts.append(gain_s)
        return grad_mixed

    def through_attention(s, grad_mixed):
        query_s, kv_terms = step(
            attend_back,
            query_low,
            kv_pieces,
            limits,
            lse[s],
            mixed[s],
            grad_mixed,
            q_cos,
            q_sin,
            bases,
            s,
        )
        grad_query.append(query_s)
        return lax.all_to_all(kv_terms, "ctx", 0, 0, tiled=True)

    def to_owners(s, parts):
        kv_s, part_s = step(project_back, grad_query[s], parts, kv_cos, kv_sin, attn_full)
        grad_kv.append(kv_s)
        return exchange(part_s, "tp")

    def through_norm(s, pieces):
        rows_s = lax.dynamic_slice_in_dim(rows_in, s * toks + tp * block, block, 0)
        wide_s = lax.dynamic_slice_in_dim(grad_wide[s], tp * block, block, 0)
        grad_s, gain_s = step(grad_inputs_of, rows_s, wide_s, gain_one, pieces)
        gain_one_parts.append(gain_s)
        grad_pieces.append(partners(grad_s, "tp"))

    out_far, terms, pieces = out_near, None, None
    for s in seqs:
        grad_mixed = through_middle(s)
        if s > 0:
            pieces = to_owners(s - 1, terms)
        terms = through_attention(s, grad_mixed)
        if s == 0 and n_tp > 1:
            out_far = swap(after(out_near, grad_query[0]), "tp", 1)
        if 0 < s < n_seqs - 1:
            through_norm(s - 1, pieces)
    ffn_grads = weight_grad(
        normed_two,
        [grad_rows[i * toks : (i + 1) * toks] for i in seqs],
        [after(kept[0], *last), *kept[1:]],
        2 * hidden,
        256,
    )
    last[:] = [ffn_grads]
    ffn_grads = lax.psum_scatter(ffn_grads, both, scatter_dimension=0, tiled=True)
    held, pieces = pieces, to_owners(n_seqs - 1, terms)
    if n_seqs > 1:
        through_norm(n_seqs - 2, held)
    grad_attn[0] = after(grad_attn[0], out_far, *last)
    attn_grads = weight_grad(
        [normed_one[s * toks : (s + 1) * toks] for s in seqs],
        grad_attn,
        [jnp.concatenate([grad_query[s], grad_kv[s], mixed[s]], axis=1) for s in seqs],
        qkv_width,
        384,
    )
    last[:] = [attn_grads]
    attn_grads = lax.psum_scatter(
        after(attn_grads, ffn_grads), both, scatter_dimension=0, tiled=True
    ).astype(F32)
    through_norm(n_seqs - 1, pieces)
    grads = [place(pieces, "tp", 0) for pieces in grad_pieces]
    gain_one_parts[0] = after(gain_one_parts[0], grad_pieces[-1][min(1, n_tp - 1)])

    total = jnp.concatenate(middle, axis=0) + out_near.astype(F32)
    if n_tp > 1:
        total = total + out_far.astype(F32)
    result = total.astype(BF16).reshape(n_seqs, toks, width)

    gain_grads = jnp.concatenate(
        [sum_over(sum(gain_one_parts), "tp"), sum(gain_two_parts)], axis=0
    )
    for axis in both:
        gain_grads = sum_over(gain_grads, axis)
    part = lax.axis_index("shard") * n_ctx + ctx
    gain_grads = lax.dynamic_slice_in_dim(gain_grads, part * own_rows, own_rows, 1)
    return (
        result,
        jnp.stack(grads),
        gain_grads[0],
        attn_grads[:, :q_width],
        attn_grads[:, q_width : q_width + kv_width],
        attn_grads[:, q_width + kv_width : qkv_width],
        attn_grads[:, qkv_width:].T,
        gain_grads[1],
        ffn_grads[:, :hidden].astype(F32),
        ffn_grads[:, hidden : 2 * hidden].astype(F32),
        ffn_grads[:, 2 * hidden :].T.astype(F32),
    )


def solution(mesh):
    both = ("shard", "ctx")
    rows = P("shard", "ctx", None)
    return jax.shard_map(
        local,
        mesh=mesh,
        in_specs=(
            rows,
            P("shard", None),
            P(both),
            P(both, "tp"),
            P(both, "tp"),
            P(both, "tp"),
            P("tp", both),
            P(both),
            P(both, "tp"),
            P(both, "tp"),
            P("tp", both),
            rows,
        ),
        out_specs=(
            rows,
            rows,
            P(both),
            P(both, "tp"),
            P(both, "tp"),
            P(both, "tp"),
            P("tp", both),
            P(both),
            P(both, "tp"),
            P(both, "tp"),
            P("tp", both),
        ),
        check_vma=False,
    )
```

```python
import functools
import math

import jax
import jax.numpy as jnp
from jax import lax
from jax.experimental import pallas as pl
from jax.experimental.pallas import tpu as pltpu
from jax.sharding import PartitionSpec as P

HEAD_SIZE = 96
PIECE = 256

EPSILON = 1e-05
ROPE_BASE = 100000.0
NEGATIVE = -1e30
F32 = jnp.float32
BF16 = jnp.bfloat16
LANES = 128
VMEM_LIMIT = 56 << 20
TAIL = 30.0
COST_SCALE = 10


def nt(left, right):
    return lax.dot_general(left, right, (((1,), (1,)), ((), ())), preferred_element_type=F32)


def nn(left, right):
    return jnp.dot(left, right, preferred_element_type=F32)


def params():
    return pltpu.CompilerParams(vmem_limit_bytes=VMEM_LIMIT)


def cost(flops, bytes_accessed, transcendentals=0, weight=1.0):
    return pl.CostEstimate(
        flops=int(flops * COST_SCALE * weight),
        bytes_accessed=int(bytes_accessed * COST_SCALE * weight),
        transcendentals=int(transcendentals * COST_SCALE * weight),
    )


def tail_cost(*args, **kwargs):
    return cost(*args, **kwargs, weight=TAIL)


def columns(array, start, size):
    if size % LANES or start % size:
        array, start = array[:, start : start + size], 0
    return array, pl.BlockSpec((array.shape[0], size), lambda r: (0, start // size))


def turn(value, cosine, sine):
    half = HEAD_SIZE // 2
    width = value.shape[-1]
    lane = lax.broadcasted_iota(jnp.int32, (1, width), 1) % HEAD_SIZE
    other = jnp.where(
        jnp.broadcast_to(lane, value.shape) < half, pltpu.roll(value, width - half, 1), pltpu.roll(value, half, 1)
    )
    return value * cosine + other * sine


def project_kernel(q_width, rows_ref, gain_ref, weight_ref, cos_ref, sin_ref, normed_ref, q_ref, kv_ref):
    rows = rows_ref[...].astype(F32)
    inverse = lax.rsqrt(jnp.mean(rows * rows, axis=-1, keepdims=True) + EPSILON)
    normed = (rows * inverse * gain_ref[...]).astype(BF16)
    normed_ref[...] = normed
    turned = turn(nn(normed, weight_ref[...]), cos_ref[...], sin_ref[...]).astype(BF16)
    q_ref[...] = turned[:, :q_width]
    kv_ref[...] = turned[:, q_width:]


def project(inputs, gain, weights, cosine, sine, q_width, row_tile=256):
    rows, width = inputs.shape
    out_width = cosine.shape[1]
    per_seq = cosine.shape[0] // row_tile
    table = pl.BlockSpec((row_tile, out_width), lambda r: (r % per_seq, 0))
    return pl.pallas_call(
        functools.partial(project_kernel, q_width),
        grid=(rows // row_tile,),
        in_specs=[
            pl.BlockSpec((row_tile, width), lambda r: (r, 0)),
            pl.BlockSpec((1, width), lambda r: (0, 0)),
            pl.BlockSpec((width, out_width), lambda r: (0, 0)),
            table,
            table,
        ],
        out_specs=[
            pl.BlockSpec((row_tile, width), lambda r: (r, 0)),
            pl.BlockSpec((row_tile, q_width), lambda r: (r, 0)),
            pl.BlockSpec((row_tile, out_width - q_width), lambda r: (r, 0)),
        ],
        out_shape=[
            jax.ShapeDtypeStruct((rows, width), BF16),
            jax.ShapeDtypeStruct((rows, q_width), BF16),
            jax.ShapeDtypeStruct((rows, out_width - q_width), BF16),
        ],
        compiler_params=params(),
        cost_estimate=cost(2 * rows * width * out_width, 4 * rows * width + 2 * width * out_width),
        name="project",
    )(inputs, gain, weights, cosine, sine)


def stacked(block, group, repeat):
    first = group * repeat
    return jnp.concatenate(
        [
            block[:, (first + r) * HEAD_SIZE : (first + r + 1) * HEAD_SIZE]
            for r in range(repeat)
        ],
        axis=0,
    )


def side_by_side(groups, repeat, tile):
    return jnp.concatenate(
        [g[r * tile : (r + 1) * tile] for g in groups for r in range(repeat)], axis=1
    )


def attend_kernel(n_groups, repeat, n_blocks, bases_ref, q_ref, limit_ref, *refs):
    kv_refs = refs[:n_blocks]
    mixed_ref, lse_ref, k_s, vt_s = refs[n_blocks:]
    tile = q_ref.shape[0]
    block = kv_refs[0].shape[0]
    cols = repeat * tile
    kv_width = n_groups * HEAD_SIZE
    factor = HEAD_SIZE ** (-0.5) * math.log2(math.e)

    @pl.when(pl.program_id(0) == 0)
    def _():
        for j, ref in enumerate(kv_refs):
            for g in range(n_groups):
                first = g * HEAD_SIZE
                k_s[g, j] = ref[:, first : first + HEAD_SIZE]
                vt_s[g, j] = ref[:, kv_width + first : kv_width + first + HEAD_SIZE].T

    limit = jnp.concatenate([limit_ref[0, 0]] * repeat, axis=1)
    offset = lax.broadcasted_iota(jnp.int32, (block, cols), 0)
    results = []
    for g in range(n_groups):
        q = stacked(q_ref[...], g, repeat)
        blocks = []
        for j in range(n_blocks):
            scores = nt(k_s[g, j], q) * factor
            blocks.append(jnp.where(offset <= limit - bases_ref[j], scores, NEGATIVE))
        top = functools.reduce(
            jnp.maximum, [jnp.max(x, axis=0, keepdims=True) for x in blocks]
        )
        total = jnp.zeros((1, cols), F32)
        acc = jnp.zeros((HEAD_SIZE, cols), F32)
        for j in range(n_blocks):
            probs = jnp.exp2(blocks[j] - top)
            total = total + jnp.sum(probs, axis=0, keepdims=True)
            acc = acc + nn(vt_s[g, j], probs.astype(BF16))
        lse_ref[0, g : g + 1, :] = top + jnp.log2(total)
        results.append((acc / total).T)
    mixed_ref[...] = side_by_side(results, repeat, tile).astype(BF16)


def attend(query, kv_pieces, limits, bases, seq):
    _, toks, q_width = query.shape
    n_blocks = len(kv_pieces)
    block, kv_cols = toks, kv_pieces[0].shape[1]
    n_groups = kv_cols // (2 * HEAD_SIZE)
    repeat = q_width // HEAD_SIZE // n_groups
    n_tiles = toks // TILE
    length = block * n_blocks
    return pl.pallas_call(
        functools.partial(attend_kernel, n_groups, repeat, n_blocks),
        grid_spec=pltpu.PrefetchScalarGridSpec(
            num_scalar_prefetch=1,
            grid=(n_tiles,),
            in_specs=[
                pl.BlockSpec((None, TILE, q_width), lambda t, _: (seq, t, 0)),
                pl.BlockSpec((1, 1, 1, TILE), lambda t, _: (seq, t, 0, 0)),
            ]
            + [pl.BlockSpec((block, kv_cols), lambda t, _: (seq, 0))] * n_blocks,
            out_specs=[
                pl.BlockSpec((TILE, q_width), lambda t, _: (t, 0)),
                pl.BlockSpec((1, n_groups, repeat * TILE), lambda t, _: (t, 0, 0)),
            ],
            scratch_shapes=[
                pltpu.VMEM((n_groups, n_blocks, block, HEAD_SIZE), BF16),
                pltpu.VMEM((n_groups, n_blocks, HEAD_SIZE, block), BF16),
            ],
        ),
        out_shape=[
            jax.ShapeDtypeStruct((toks, q_width), BF16),
            jax.ShapeDtypeStruct((n_tiles, n_groups, repeat * TILE), F32),
        ],
        compiler_params=params(),
        cost_estimate=cost(
            4 * toks * length * 256 * n_groups * repeat,
            4 * toks * q_width + 2 * length * kv_cols,
            toks * length * n_groups * repeat,
        ),
        name="attend",
    )(bases, query, limits, *kv_pieces)


def attend_back_kernel(n_groups, repeat, n_blocks, bases_ref, q_ref, limit_ref, lse_ref, mixed_ref, grad_ref, cos_ref, sin_ref, *refs):
    kv_refs, refs = refs[:n_blocks], refs[n_blocks:]
    dq_ref, dkv_ref, k_s, v_s, kt_s, dk_s, dv_s = refs
    tile = q_ref.shape[0]
    block = kv_refs[0].shape[0]
    cols = repeat * tile
    kv_width = n_groups * HEAD_SIZE
    scale = HEAD_SIZE ** (-0.5)
    factor = scale * math.log2(math.e)

    @pl.when(pl.program_id(0) == 0)
    def _():
        for j, ref in enumerate(kv_refs):
            for g in range(n_groups):
                first = g * HEAD_SIZE
                k = ref[:, first : first + HEAD_SIZE]
                k_s[g, j] = k
                kt_s[g, j] = k.T
                v_s[g, j] = ref[:, kv_width + first : kv_width + first + HEAD_SIZE]
        dk_s[...] = jnp.zeros_like(dk_s)
        dv_s[...] = jnp.zeros_like(dv_s)

    limit = jnp.concatenate([limit_ref[0, 0]] * repeat, axis=1)
    offset = lax.broadcasted_iota(jnp.int32, (block, cols), 0)
    ones = jnp.ones((8, HEAD_SIZE), BF16)
    results = []
    for g in range(n_groups):
        q = stacked(q_ref[...], g, repeat)
        grad = stacked(grad_ref[...], g, repeat)
        mixed = stacked(mixed_ref[...], g, repeat)
        product = grad.astype(F32) * mixed.astype(F32)
        high = product.astype(BF16)
        low = (product - high.astype(F32)).astype(BF16)
        delta = (nt(ones, high) + nt(ones, low))[0:1]
        lse = lse_ref[0, g : g + 1, :]
        dqt = jnp.zeros((HEAD_SIZE, cols), F32)
        for j in range(n_blocks):
            scores = nt(k_s[g, j], q) * factor - lse
            probs = jnp.where(offset <= limit - bases_ref[j], jnp.exp2(scores), 0.0)
            grad_soft = nt(v_s[g, j], grad)
            grad_scores = (probs * (grad_soft - delta)).astype(BF16)
            dv_s[g, j] += nn(probs.astype(BF16), grad)
            dk_s[g, j] += nn(grad_scores, q)
            dqt = dqt + nn(kt_s[g, j], grad_scores)
        results.append(dqt.T * scale)
    dq_ref[...] = turn(side_by_side(results, repeat, tile), cos_ref[...], -sin_ref[...]).astype(BF16)

    @pl.when(pl.program_id(0) == pl.num_programs(0) - 1)
    def _():
        for j in range(n_blocks):
            rows = pl.ds(pl.multiple_of(bases_ref[j], block), block)
            dkv_ref[rows, :] = jnp.concatenate(
                [(dk_s[g, j] * scale).astype(BF16) for g in range(n_groups)]
                + [dv_s[g, j].astype(BF16) for g in range(n_groups)],
                axis=1,
            )


def attend_back(query, kv_pieces, limits, lse, mixed, grad, cosine, sine, bases, seq):
    _, toks, q_width = query.shape
    n_blocks = len(kv_pieces)
    block, kv_cols = toks, kv_pieces[0].shape[1]
    n_groups = kv_cols // (2 * HEAD_SIZE)
    repeat = q_width // HEAD_SIZE // n_groups
    n_tiles = toks // TILE
    length = block * n_blocks
    rows = pl.BlockSpec((TILE, q_width), lambda t, _: (t, 0))
    kv_piece = pl.BlockSpec((block, kv_cols), lambda t, _: (seq, 0))
    return pl.pallas_call(
        functools.partial(attend_back_kernel, n_groups, repeat, n_blocks),
        grid_spec=pltpu.PrefetchScalarGridSpec(
            num_scalar_prefetch=1,
            grid=(n_tiles,),
            in_specs=[
                pl.BlockSpec((None, TILE, q_width), lambda t, _: (seq, t, 0)),
                pl.BlockSpec((1, 1, 1, TILE), lambda t, _: (seq, t, 0, 0)),
                pl.BlockSpec((1, n_groups, repeat * TILE), lambda t, _: (t, 0, 0)),
                rows,
                rows,
                rows,
                rows,
            ]
            + [kv_piece] * n_blocks,
            out_specs=[rows, pl.BlockSpec((length, kv_cols), lambda t, _: (0, 0))],
            scratch_shapes=[
                pltpu.VMEM((n_groups, n_blocks, block, HEAD_SIZE), BF16),
                pltpu.VMEM((n_groups, n_blocks, block, HEAD_SIZE), BF16),
                pltpu.VMEM((n_groups, n_blocks, HEAD_SIZE, block), BF16),
                pltpu.VMEM((n_groups, n_blocks, block, HEAD_SIZE), F32),
                pltpu.VMEM((n_groups, n_blocks, block, HEAD_SIZE), F32),
            ],
        ),
        out_shape=[
            jax.ShapeDtypeStruct((toks, q_width), BF16),
            jax.ShapeDtypeStruct((length, kv_cols), BF16),
        ],
        compiler_params=params(),
        cost_estimate=tail_cost(
            10 * toks * length * 256 * n_groups * repeat,
            8 * toks * q_width + 4 * length * kv_cols,
            toks * length * n_groups * repeat,
        ),
        name="attend_back",
    )(bases, query, limits, lse, mixed, grad, cosine, sine, *kv_pieces)


def project_back_kernel(query_ref, cos_ref, sin_ref, weight_ref, terms_ref, kv_ref, part_ref):
    total = jnp.sum(terms_ref[...].astype(F32), axis=0)
    kv = turn(total, cos_ref[...], -sin_ref[...]).astype(BF16)
    kv_ref[...] = kv
    both = jnp.concatenate([query_ref[...], kv], axis=1)
    part_ref[...] = nt(both, weight_ref[...]).astype(BF16)


def project_back(query, terms, cosine, sine, weights):
    toks, kv_cols = cosine.shape
    count = terms.shape[0] // toks
    width, columns = weights.shape[0], query.shape[1] + kv_cols

    def whole(rows, cols):
        return pl.BlockSpec((rows, cols), lambda r: (0, 0))

    return pl.pallas_call(
        project_back_kernel,
        grid=(1,),
        in_specs=[
            whole(*query.shape),
            whole(toks, kv_cols),
            whole(toks, kv_cols),
            whole(width, columns),
            pl.BlockSpec((count, toks, kv_cols), lambda r: (0, 0, 0)),
        ],
        out_specs=[whole(toks, kv_cols), whole(toks, width)],
        out_shape=[
            jax.ShapeDtypeStruct((toks, kv_cols), BF16),
            jax.ShapeDtypeStruct((toks, width), BF16),
        ],
        compiler_params=params(),
        cost_estimate=tail_cost(
            2 * toks * width * columns, 2 * width * (toks + columns)
        ),
        name="project_back",
    )(query, cosine, sine, weights, terms.reshape(count, toks, kv_cols))


def middle_kernel(count, rows_ref, gain_ref, weight_ref, *refs):
    middle_ref, normed_ref = refs[count:]
    mixed = jnp.concatenate([ref[...] for ref in refs[:count]], axis=1)
    middle = rows_ref[...].astype(F32) + nt(mixed, weight_ref[...])
    inverse = lax.rsqrt(jnp.mean(middle * middle, axis=-1, keepdims=True) + EPSILON)
    middle_ref[...] = middle
    normed_ref[...] = (middle * inverse * gain_ref[...]).astype(BF16)


def middle_of(inputs, gain, weights, start, pieces, seq, row_tile=256):
    width = inputs.shape[1]
    toks, q_width = pieces[0].shape
    steps = toks // row_tile
    rows = pl.BlockSpec((row_tile, width), lambda r: (r, 0))
    weights, weight_spec = columns(weights, start, q_width * len(pieces))
    return pl.pallas_call(
        functools.partial(middle_kernel, len(pieces)),
        grid=(steps,),
        in_specs=[
            pl.BlockSpec((row_tile, width), lambda r: (seq * steps + r, 0)),
            pl.BlockSpec((1, width), lambda r: (0, 0)),
            weight_spec,
        ]
        + [pl.BlockSpec((row_tile, q_width), lambda r: (r, 0))] * len(pieces),
        out_specs=[rows, rows],
        out_shape=[
            jax.ShapeDtypeStruct((toks, width), F32),
            jax.ShapeDtypeStruct((toks, width), BF16),
        ],
        compiler_params=params(),
        cost_estimate=cost(
            2 * toks * width * width, 10 * toks * width + 2 * width * width
        ),
        name="middle_of",
    )(inputs, gain, weights, *pieces)


def ffn_kernel(keep, based, groups, normed_ref, grad_ref, *refs):
    weight_refs, refs = refs[: 3 * groups], refs[3 * groups :]
    normed, grad = normed_ref[...], grad_ref[...]
    out = back = None
    if based:
        out, back = refs[0][...].astype(F32), refs[1][...].astype(F32)
        refs = refs[2:]
    for g in range(groups):
        gate_w, up_w, down_w = [ref[...] for ref in weight_refs[3 * g : 3 * g + 3]]
        gate = nn(normed, gate_w)
        up = nn(normed, up_w)
        grad_hidden = nn(grad, down_w)
        sig = jax.nn.sigmoid(gate)
        silu = gate * sig
        hidden = (silu * up).astype(BF16)
        grad_gate = (grad_hidden * up * (sig + silu * (1.0 - sig))).astype(BF16)
        grad_up = (grad_hidden * silu).astype(BF16)
        out_g = nt(hidden, down_w)
        back_g = nt(grad_gate, gate_w) + nt(grad_up, up_w)
        out = out_g if out is None else out + out_g
        back = back_g if back is None else back + back_g
        if keep and g == 0:
            refs[2][...] = jnp.concatenate([grad_gate, grad_up, hidden], axis=1)
    refs[0][...] = out.astype(BF16)
    refs[1][...] = back.astype(BF16)


def ffn_groups(normed, grad, weights, hidden, seq, base, keep, row_tile=256):
    toks, width = normed.shape
    steps = toks // row_tile
    groups = len(weights)
    rows = pl.BlockSpec((row_tile, width), lambda r: (r, 0))
    kept = pl.BlockSpec((row_tile, 3 * hidden), lambda r: (r, 0))
    wide = jax.ShapeDtypeStruct((toks, width), BF16)
    return pl.pallas_call(
        functools.partial(ffn_kernel, keep, bool(base), groups),
        grid=(steps,),
        in_specs=[rows, pl.BlockSpec((row_tile, width), lambda r: (seq * steps + r, 0))]
        + [
            pl.BlockSpec((width, hidden), lambda r, c=c: (0, c), pipeline_mode=pl.Buffered(1))
            for _ in weights
            for c in range(3)
        ]
        + [rows] * len(base),
        out_specs=[rows, rows] + [kept] * int(keep),
        out_shape=[wide, wide] + [jax.ShapeDtypeStruct((toks, 3 * hidden), BF16)] * int(keep),
        compiler_params=params(),
        cost_estimate=cost(
            12 * groups * toks * width * hidden,
            8 * toks * width + 6 * groups * width * hidden,
            groups * toks * hidden,
        ),
        name="ffn_groups",
    )(normed, grad, *[w for w in weights for _ in range(3)], *base)


def grad_middle_kernel(count, middle_ref, grad_ref, gain_ref, weight_ref, *refs):
    wide_ref, attn_ref, mixed_ref, gain_grad_ref = refs[count:]
    middle = middle_ref[...]
    inverse = lax.rsqrt(jnp.mean(middle * middle, axis=-1, keepdims=True) + EPSILON)
    hat = middle * inverse
    back = refs[0][...].astype(F32)
    for ref in refs[1:count]:
        back = back + ref[...].astype(F32)
    scaled = back * gain_ref[...]
    total = grad_ref[...].astype(F32) + inverse * (
        scaled - hat * jnp.mean(scaled * hat, axis=-1, keepdims=True)
    )
    wide_ref[...] = total
    attn = total.astype(BF16)
    attn_ref[...] = attn
    mixed_ref[...] = nn(attn, weight_ref[...]).astype(BF16)
    part = jnp.sum(back * hat, axis=0, keepdims=True)

    @pl.when(pl.program_id(0) == 0)
    def _():
        gain_grad_ref[...] = part

    @pl.when(pl.program_id(0) > 0)
    def _():
        gain_grad_ref[...] += part


def grad_middle_of(middle, grad, gain, weights, start, backs, q_width, seq, row_tile=256):
    toks, width = middle.shape
    steps = toks // row_tile
    rows = pl.BlockSpec((row_tile, width), lambda r: (r, 0))
    line = pl.BlockSpec((1, width), lambda r: (0, 0))
    weights, weight = columns(weights, start, q_width)
    return pl.pallas_call(
        functools.partial(grad_middle_kernel, len(backs)),
        grid=(steps,),
        in_specs=[
            rows,
            pl.BlockSpec((row_tile, width), lambda r: (seq * steps + r, 0)),
            line,
            weight,
        ]
        + [rows] * len(backs),
        out_specs=[rows, rows, pl.BlockSpec((row_tile, q_width), lambda r: (r, 0)), line],
        out_shape=[
            jax.ShapeDtypeStruct((toks, width), F32),
            jax.ShapeDtypeStruct((toks, width), BF16),
            jax.ShapeDtypeStruct((toks, q_width), BF16),
            jax.ShapeDtypeStruct((1, width), F32),
        ],
        compiler_params=params(),
        cost_estimate=tail_cost(2 * toks * width * q_width, 16 * toks * width),
        name="grad_middle_of",
    )(middle, grad, gain, weights, *backs)


def weight_grad_kernel(n_seqs, tile, split, *refs):
    lefts, others, rights = refs[:n_seqs], refs[n_seqs : 2 * n_seqs], refs[2 * n_seqs : 3 * n_seqs]
    out_ref, left_s, other_s = refs[3 * n_seqs :]
    toks = lefts[0].shape[0]

    @pl.when(pl.program_id(0) == 0)
    def _():
        for s in range(n_seqs):
            left_s[:, s * toks : (s + 1) * toks] = lefts[s][...].T
            other_s[:, s * toks : (s + 1) * toks] = others[s][...].T

    right = jnp.concatenate([ref[...] for ref in rights], axis=0)
    if split % tile:
        out_ref[...] = jnp.concatenate(
            [nn(left_s[...], right[:, :split]), nn(other_s[...], right[:, split:])], axis=1
        ).astype(BF16)
        return
    first = pl.program_id(0) < split // tile

    @pl.when(first)
    def _():
        out_ref[...] = nn(left_s[...], right).astype(BF16)

    @pl.when(jnp.logical_not(first))
    def _():
        out_ref[...] = nn(other_s[...], right).astype(BF16)


def weight_grad(lefts, others, rights, split, tile):
    toks, width = lefts[0].shape
    columns = rights[0].shape[1]
    if tile % LANES or columns % tile or split % tile:
        tile = columns
    n_seqs = len(lefts)
    whole = pl.BlockSpec((toks, width), lambda c: (0, 0))
    return pl.pallas_call(
        functools.partial(weight_grad_kernel, n_seqs, tile, split),
        grid=(columns // tile,),
        in_specs=[whole] * (2 * n_seqs)
        + [pl.BlockSpec((toks, tile), lambda c: (0, c))] * n_seqs,
        out_specs=pl.BlockSpec((width, tile), lambda c: (0, c)),
        out_shape=jax.ShapeDtypeStruct((width, columns), BF16),
        scratch_shapes=[pltpu.VMEM((width, n_seqs * toks), BF16)] * 2,
        compiler_params=params(),
        cost_estimate=tail_cost(
            2 * n_seqs * toks * width * columns,
            2 * n_seqs * toks * (2 * width + columns) + 2 * width * columns,
        ),
        name="weight_grad",
    )(*lefts, *others, *rights)


def grad_inputs_kernel(rows_ref, wide_ref, gain_ref, *refs):
    *term_refs, out_ref, gain_grad_ref = refs
    rows = rows_ref[...].astype(F32)
    inverse = lax.rsqrt(jnp.mean(rows * rows, axis=-1, keepdims=True) + EPSILON)
    hat = rows * inverse
    back = term_refs[0][...].astype(F32)
    for ref in term_refs[1:]:
        back = back + ref[...].astype(F32)
    scaled = back * gain_ref[...]
    total = wide_ref[...] + inverse * (
        scaled - hat * jnp.mean(scaled * hat, axis=-1, keepdims=True)
    )
    out_ref[...] = total.astype(BF16)
    gain_grad_ref[...] = jnp.sum(back * hat, axis=0, keepdims=True)


def grad_inputs_of(inputs, wide, gain, terms):
    toks, width = inputs.shape
    return pl.pallas_call(
        grad_inputs_kernel,
        out_shape=[
            jax.ShapeDtypeStruct((toks, width), BF16),
            jax.ShapeDtypeStruct((1, width), F32),
        ],
        compiler_params=params(),
        cost_estimate=tail_cost(0, 16 * toks * width),
        name="grad_inputs_of",
    )(inputs, wide, gain, *terms)


TILE = 128


def rotation_tables(positions, turned, plain):
    half = HEAD_SIZE // 2
    lane = jnp.arange((turned + plain) * HEAD_SIZE, dtype=jnp.int32)
    inverse = jnp.exp(
        (lane % half).astype(F32) * (-2.0 * math.log(ROPE_BASE) / HEAD_SIZE)
    )
    turns = lane < turned * HEAD_SIZE
    angles = positions.astype(F32)[:, None] * inverse[None, :]
    sign = jnp.where(turns, jnp.where(lane % HEAD_SIZE < half, -1.0, 1.0), 0.0)
    return jnp.where(turns, jnp.cos(angles), 1.0), jnp.sin(angles) * sign


def last_allowed(positions, start_row):
    begin = start_row[:, None, :]
    inside = (positions[None, :, None] >= begin) & (positions[None, :, None] < begin + PIECE)
    ends = jnp.where(inside, begin + PIECE - 1, -1)
    return jnp.maximum(positions[None, :], jnp.max(ends, axis=-1)).astype(jnp.int32)


def swap(value, axis, step):
    count = lax.axis_size(axis)
    return lax.ppermute(value, axis, [(i, i ^ step) for i in range(count)])


def partners(value, axis):
    return [value] + [swap(value, axis, j) for j in range(1, lax.axis_size(axis))]


def place(pieces, axis, dim):
    me = lax.axis_index(axis)
    width = pieces[0].shape[dim]
    shape = list(pieces[0].shape)
    shape[dim] = width * len(pieces)
    whole = jnp.zeros(shape, pieces[0].dtype)
    for j, piece in enumerate(pieces):
        whole = lax.dynamic_update_slice_in_dim(whole, piece, (me ^ j) * width, dim)
    return whole


def exchange(value, axis):
    me = lax.axis_index(axis)
    count = lax.axis_size(axis)
    size = value.shape[0] // count
    blocks = [lax.dynamic_slice_in_dim(value, (me ^ j) * size, size, 0) for j in range(count)]
    return [blocks[0]] + [swap(blocks[j], axis, j) for j in range(1, count)]


def after(value, *others):
    return lax.optimization_barrier((value, *others))[0]


def sum_over(value, axis):
    pieces = partners(value, axis)
    return sum(pieces[1:], pieces[0])


def local(
    inputs,
    starts,
    first_gain,
    query_weight,
    key_matrix,
    value_matrix,
    out_weight,
    second_gain,
    gate_weight,
    up_weight,
    down_weight,
    grad_out,
):
    n_seqs, toks, width = inputs.shape
    q_width = query_weight.shape[1]
    kv_width = key_matrix.shape[1]
    qkv_width = q_width + 2 * kv_width
    turned = (q_width + kv_width) // HEAD_SIZE
    own_rows = query_weight.shape[0]
    hidden = gate_weight.shape[1]
    n_ctx = lax.axis_size("ctx")
    n_tp = lax.axis_size("tp")
    ctx = lax.axis_index("ctx")
    tp = lax.axis_index("tp")
    both = ("shard", "ctx")
    seqs = range(n_seqs)
    block = toks // n_tp

    def gather(value):
        return lax.all_gather(value, both, axis=0, tiled=True)

    last = []

    def step(kernel, first, *rest, **kwargs):
        out = kernel(after(first, *last) if last else first, *rest, **kwargs)
        last[:] = [out[0] if isinstance(out, (list, tuple)) else out]
        return out

    gains_own = jnp.concatenate(
        [
            first_gain[:, None],
            second_gain[:, None],
            jnp.zeros((own_rows, LANES - 2), BF16),
        ],
        axis=1,
    )
    qkv_own = jnp.concatenate([query_weight, key_matrix, value_matrix], axis=1)
    attn_own = jnp.concatenate([qkv_own, gains_own], axis=1)
    query_pos = ctx * toks + jnp.arange(toks, dtype=jnp.int32)
    bases = jnp.stack([(ctx ^ j) * toks for j in range(n_ctx)]).astype(jnp.int32)
    limits = last_allowed(query_pos, starts).reshape(n_seqs, toks // TILE, 1, TILE)
    cosine, sine = rotation_tables(query_pos, turned, kv_width // HEAD_SIZE)
    attn_pieces = partners(attn_own, "ctx")
    out_pieces = partners(out_weight.T, "tp")
    attn_part = place(attn_pieces, "ctx", 0)
    attn_part, cosine, sine, *out_pieces = lax.optimization_barrier(
        (attn_part, cosine, sine, *out_pieces)
    )
    attn_full = place(partners(attn_part, "shard"), "shard", 0)
    gain_one = attn_full[:, qkv_width].astype(F32)[None, :]
    gain_two = attn_full[:, qkv_width + 1].astype(F32)[None, :]

    ffn_own = jnp.concatenate([gate_weight, up_weight, down_weight.T], axis=1)
    own_full = gather(jnp.concatenate([ffn_own, *out_pieces], axis=1))
    out_start = 3 * hidden
    ffn_far = [swap(after(ffn_own, *attn_pieces), "tp", j) for j in range(2, n_tp, 2)]

    rows_in = inputs.reshape(n_seqs * toks, width)
    grad_rows = grad_out.reshape(n_seqs * toks, width)
    normed_one, query_low, kv_own = step(
        project, rows_in, gain_one, attn_full, cosine, sine, q_width
    )
    query_low = query_low.reshape(n_seqs, toks, q_width)

    kv_pieces = partners(kv_own, "ctx")
    mixed, lse, mixed_all = [], [], []
    ffn_weights = [own_full]
    for s in seqs:
        mixed_s, lse_s = step(attend, query_low, kv_pieces, limits, bases, s)
        mixed.append(mixed_s)
        lse.append(lse_s)
        mixed_all.append(partners(mixed_s, "tp"))
        if s == 0:
            ffn_weights += [gather(after(far, mixed_s)) for far in ffn_far]

    middle, normed_two, out_terms, backs, kept = [], [], [], [], []
    for s in seqs:
        middle_s, normed_s = step(middle_of, rows_in, gain_two, own_full, out_start, mixed_all[s], s)
        terms = ()
        batches = [ffn_weights] if s else [ffn_weights[:1]] + [[w] for w in ffn_weights[1:]]
        for j, weights in enumerate(batches):
            terms = step(ffn_groups, normed_s, grad_rows, weights, hidden, s, terms, j == 0)
            if j == 0:
                kept.append(terms[2])
                terms = terms[:2]
        middle.append(middle_s)
        normed_two.append(normed_s)
        out_terms.append(terms[0])
        backs.append([terms[1]] + ([swap(terms[1], "tp", 1)] if n_tp > 1 else []))
    out_near = jnp.concatenate(out_terms, axis=0)

    grad_wide, grad_attn, grad_query, grad_kv, gain_two_parts = [], [], [], [], []
    grad_pieces, gain_one_parts = [], []
    q_cos, q_sin = cosine[:, :q_width], sine[:, :q_width]
    kv_cos, kv_sin = cosine[:, q_width:], sine[:, q_width:]

    def through_middle(s):
        wide_s, attn_s, grad_mixed, gain_s = step(
            grad_middle_of, middle[s], grad_rows, gain_two, own_full, out_start, backs[s], q_width, s
        )
        grad_wide.append(wide_s)
        grad_attn.append(attn_s)
        gain_two_parts.append(gain_s)
        return grad_mixed

    def through_attention(s, grad_mixed):
        query_s, kv_terms = step(
            attend_back,
            query_low,
            kv_pieces,
            limits,
            lse[s],
            mixed[s],
            grad_mixed,
            q_cos,
            q_sin,
            bases,
            s,
        )
        grad_query.append(query_s)
        return lax.all_to_all(kv_terms, "ctx", 0, 0, tiled=True)

    def to_owners(s, parts):
        kv_s, part_s = step(project_back, grad_query[s], parts, kv_cos, kv_sin, attn_full)
        grad_kv.append(kv_s)
        return exchange(part_s, "tp")

    def through_norm(s, pieces):
        rows_s = lax.dynamic_slice_in_dim(rows_in, s * toks + tp * block, block, 0)
        wide_s = lax.dynamic_slice_in_dim(grad_wide[s], tp * block, block, 0)
        grad_s, gain_s = step(grad_inputs_of, rows_s, wide_s, gain_one, pieces)
        gain_one_parts.append(gain_s)
        grad_pieces.append(partners(grad_s, "tp"))

    out_far, terms, pieces = out_near, None, None
    for s in seqs:
        grad_mixed = through_middle(s)
        if s > 0:
            pieces = to_owners(s - 1, terms)
        terms = through_attention(s, grad_mixed)
        if s == 0 and n_tp > 1:
            out_far = swap(after(out_near, grad_query[0]), "tp", 1)
        if 0 < s < n_seqs - 1:
            through_norm(s - 1, pieces)
    ffn_grads = weight_grad(
        normed_two,
        [grad_rows[i * toks : (i + 1) * toks] for i in seqs],
        [after(kept[0], *last), *kept[1:]],
        2 * hidden,
        256,
    )
    last[:] = [ffn_grads]
    ffn_grads = lax.psum_scatter(ffn_grads, both, scatter_dimension=0, tiled=True)
    held, pieces = pieces, to_owners(n_seqs - 1, terms)
    if n_seqs > 1:
        through_norm(n_seqs - 2, held)
    grad_attn[0] = after(grad_attn[0], *last)
    attn_grads = weight_grad(
        [normed_one[s * toks : (s + 1) * toks] for s in seqs],
        grad_attn,
        [jnp.concatenate([grad_query[s], grad_kv[s], mixed[s]], axis=1) for s in seqs],
        qkv_width,
        384,
    )
    last[:] = [attn_grads]
    attn_grads = lax.psum_scatter(
        after(attn_grads, ffn_grads), both, scatter_dimension=0, tiled=True
    ).astype(F32)
    through_norm(n_seqs - 1, pieces)
    grads = [place(pieces, "tp", 0) for pieces in grad_pieces]
    gain_one_parts[0] = after(gain_one_parts[0], grad_pieces[-1][min(1, n_tp - 1)])

    total = jnp.concatenate(middle, axis=0) + out_near.astype(F32)
    if n_tp > 1:
        total = total + out_far.astype(F32)
    result = total.astype(BF16).reshape(n_seqs, toks, width)

    gain_grads = jnp.concatenate(
        [sum_over(sum(gain_one_parts), "tp"), sum(gain_two_parts)], axis=0
    )
    for axis in both:
        gain_grads = sum_over(gain_grads, axis)
    part = lax.axis_index("shard") * n_ctx + ctx
    gain_grads = lax.dynamic_slice_in_dim(gain_grads, part * own_rows, own_rows, 1)
    return (
        result,
        jnp.stack(grads),
        gain_grads[0],
        attn_grads[:, :q_width],
        attn_grads[:, q_width : q_width + kv_width],
        attn_grads[:, q_width + kv_width : qkv_width],
        attn_grads[:, qkv_width:].T,
        gain_grads[1],
        ffn_grads[:, :hidden].astype(F32),
        ffn_grads[:, hidden : 2 * hidden].astype(F32),
        ffn_grads[:, 2 * hidden :].T.astype(F32),
    )


def solution(mesh):
    both = ("shard", "ctx")
    rows = P("shard", "ctx", None)
    return jax.shard_map(
        local,
        mesh=mesh,
        in_specs=(
            rows,
            P("shard", None),
            P(both),
            P(both, "tp"),
            P(both, "tp"),
            P(both, "tp"),
            P("tp", both),
            P(both),
            P(both, "tp"),
            P(both, "tp"),
            P("tp", both),
            rows,
        ),
        out_specs=(
            rows,
            rows,
            P(both),
            P(both, "tp"),
            P(both, "tp"),
            P(both, "tp"),
            P("tp", both),
            P(both),
            P(both, "tp"),
            P(both, "tp"),
            P("tp", both),
        ),
        check_vma=False,
    )
```
